128 devices in a mesh: mem: 2 (over z_lo), tile: 64 (over y, x, z_hi, core).
Axes of the slice: x: 4, y: 4, z: 4 (z_hi: 2, z_lo: 2; z = z_hi * 2 + z_lo), core: 2. Of those that a mesh axis runs over, the one named last changes fastest.
Arguments:
- prior_members: bfloat16 [256, 10, 131072], P('mem', None, 'tile'), may hold values from -6 to 6
- members_in_reading_space: bfloat16 [256, 524288], P('mem', 'tile'), may hold values from -6 to 6
- measured_values: float32 [524288], P('tile'), may hold values from -6 to 6
- obs_precision_weights: float32 [524288], P('tile'), may hold values from 0.5 to 4
- valid_reading_numbers: int32 [4096], P('tile'), may hold values from 1 to 128, as said below
- neighbour_lists: int32 [1024, 8], P('tile'), may hold values from 0 to 4095, as said below
Outputs:
- analysis: bfloat16 [256, 10, 131072], P('mem', None, 'tile')
The draws below stay inside these ranges and needn't reach their ends.
Inputs may be any that keep to these rules, and one draw needn't show every extreme that they name: `valid_reading_numbers`: every block count is at least 1; some block has 128 valid observations and some has 1. `neighbour_lists`: each row lists 8 different observation blocks. Column block b lies on tile b // 16; every block it lists lies on that tile or on one of the two tiles beside it, that is, in blocks (b // 16 - 1) * 64 to (b // 16 + 2) * 64 - 1.
All inputs are finite; a program needn't handle non-finite values.
Results may differ from the reference program's by a relative error of at most 0.0064.
Values may be sent and summed in bfloat16 or wider, within the bound.
No kernel may reach another device: no remote copies, remote signals or barrier semaphores. Data moves between devices by JAX's collectives and lax.ppermute only.
A program may use at most 128 MiB of HBM per device.

```python
import math
import jax
import jax.numpy as jnp
from jax import lax

MEMBER_NUMBER = 256
HEIGHT_LAYERS = 10
CBW = 128
OBW = 128
NLOC = 8
NSTEPS = 3
OB_DEV = 64
CB_DEV = 16
GRID_POINTS = 131072
NCB = 1024
NOB = 4096
NOBS = 524288


def draw_prior_members(key, part):
    offset_key = jax.random.fold_in(key, 3301)
    spread_key = jax.random.fold_in(key, 3302)
    offset = jax.random.uniform(offset_key, (1, HEIGHT_LAYERS, GRID_POINTS), jnp.float32, -1.0, 1.0)
    spread_part = jax.random.truncated_normal(spread_key, -5.0, 5.0, (MEMBER_NUMBER, HEIGHT_LAYERS, GRID_POINTS), jnp.float32)
    return (spread_part + offset).astype(jnp.bfloat16)


def draw_members_in_reading_space(key, part):
    leading_key = jax.random.fold_in(key, 7171)
    partner_key = jax.random.fold_in(key, 7172)
    half_count = MEMBER_NUMBER // 2
    leading = jax.random.truncated_normal(leading_key, -4.0, 4.0, (half_count, NOBS), jnp.float32)
    partner_own = jax.random.truncated_normal(partner_key, -4.0, 4.0, (half_count, NOBS), jnp.float32)
    partner = -0.6 * leading + 0.8 * partner_own
    values = jnp.concatenate([leading, partner], axis=0)
    return values.astype(jnp.bfloat16)


def draw_valid_reading_numbers(key, part):
    values = jax.random.randint(key, (NOB,), 3 * OBW // 4, OBW + 1)
    return values.at[0].set(OBW).at[NOB - 1].set(1).astype(jnp.int32)


def draw_neighbour_lists(key, part):
    ncand = 3 * OB_DEV

    def one_block(block):
        subkey = jax.random.fold_in(key, block)
        ranked = jax.random.permutation(subkey, ncand).astype(jnp.int32)
        tile_no = block // CB_DEV
        candidates = (tile_no - 1) * OB_DEV + jnp.arange(ncand, dtype=jnp.int32)
        outside = ((candidates < 0) | (candidates >= NOB)).astype(jnp.int32)
        ordering = outside * (4 * ncand) + ranked
        ordering = jnp.where((block == 0) & (candidates == 0), -1, ordering)
        ordering = jnp.where((block == NCB - 1) & (candidates == NOB - 1), -1, ordering)
        order_idx = jnp.argsort(ordering, stable=True)
        return candidates[order_idx[:NLOC]].astype(jnp.int32)
    return jax.vmap(one_block)(jnp.arange(NCB, dtype=jnp.int32))


def levels(rng, extent, shards, least, largest):
    level = 1.0
    for dim, shards_of in shards:
        heights = jax.random.uniform(jax.random.fold_in(jax.random.fold_in(rng, 6), dim), (shards_of,), jnp.float32, least / len(shards), largest / len(shards))
        level = level * jnp.repeat(jnp.exp(heights), extent[dim] // shards_of).reshape((-1,) + (1,) * (len(extent) - 1 - dim))
    return level


def centred(rng, shape, deviation, bound, shards=(), kind=jnp.bfloat16):
    entries = jax.random.normal(rng, shape, jnp.float32) * deviation
    if len(shards) > 0:
        entries = levels(rng, shape, shards, -0.22, 0.18) * entries
    return jnp.clip(entries, min=-bound, max=bound).astype(kind)


def setup_inputs(seed: int = 0) -> dict:
    keys = jax.random.split(jax.random.key(seed), 7)
    return {
        "prior_members": draw_prior_members(jax.random.fold_in(keys[6], 71), 0),
        "members_in_reading_space": draw_members_in_reading_space(jax.random.fold_in(keys[6], 71), 0),
        "measured_values": centred(keys[2], (NOBS,), 1.0, 6.0, ((0, 64),), jnp.float32),
        "obs_precision_weights": jnp.clip(jnp.exp(math.log(4.0) - 2.0794415 * jax.random.uniform(keys[3], (NOBS,), jnp.float32) ** levels(keys[3], (NOBS,), ((0, 64),), -0.2, 0.2)), 0.5, 4.0),
        "valid_reading_numbers": draw_valid_reading_numbers(jax.random.fold_in(keys[6], 71), 0),
        "neighbour_lists": draw_neighbour_lists(jax.random.fold_in(keys[6], 71), 0),
    }


def newton_block(matrix):
    order = matrix.shape[0]
    eye = jnp.eye(order, dtype=jnp.float32)
    scale = jnp.trace(matrix) / order
    iterate = matrix / scale
    inverse_root = eye
    for step in range(NSTEPS):
        factor = 1.5 * eye - 0.5 * jnp.dot(inverse_root, iterate, precision=lax.Precision.HIGHEST)
        iterate = jnp.dot(iterate, factor, precision=lax.Precision.HIGHEST)
        inverse_root = jnp.dot(factor, inverse_root, precision=lax.Precision.HIGHEST)
    return (inverse_root, scale)

def transform(ylocal, wlocal, dlocal):
    order = ylocal.shape[0]
    scaled = (ylocal.astype(jnp.float32) * wlocal).astype(jnp.bfloat16)
    matrix = (order - 1.0) * jnp.eye(order, dtype=jnp.float32) + jnp.dot(scaled, ylocal.T, preferred_element_type=jnp.float32)
    rhs = jnp.dot(scaled.astype(jnp.float32), dlocal, precision=lax.Precision.HIGHEST)
    inverse_root, scale = newton_block(matrix)
    covar = jnp.dot(inverse_root, inverse_root, precision=lax.Precision.HIGHEST) / scale
    mean_shift = jnp.dot(covar, rhs, precision=lax.Precision.HIGHEST)
    return (jnp.sqrt((order - 1.0) / scale) * inverse_root + mean_shift[:, None]).astype(jnp.bfloat16)

def reference(prior_members, members_in_reading_space, measured_values, obs_precision_weights, valid_reading_numbers, neighbour_lists):
    prior_average = lax.optimization_barrier(jnp.mean(prior_members.astype(jnp.float32), axis=0))
    prior_deviation = (prior_members.astype(jnp.float32) - prior_average).astype(jnp.bfloat16)
    ymean = lax.optimization_barrier(jnp.mean(members_in_reading_space.astype(jnp.float32), axis=0))
    ypert = (members_in_reading_space.astype(jnp.float32) - ymean).astype(jnp.bfloat16)
    innov = measured_values - ymean
    slots = jnp.arange(OBW, dtype=jnp.int32)
    valid = slots[None, :] < valid_reading_numbers[:, None]
    weight = jnp.where(valid, obs_precision_weights.reshape(NOB, OBW), 0.0)
    yblocks = ypert.reshape(MEMBER_NUMBER, NOB, OBW)
    iblocks = innov.reshape(NOB, OBW)

    def per_block(ids):
        ylocal = yblocks[:, ids].reshape(MEMBER_NUMBER, NLOC * OBW)
        return transform(ylocal, weight[ids].reshape(NLOC * OBW), iblocks[ids].reshape(NLOC * OBW))
    weights = lax.map(per_block, neighbour_lists)
    pieces = prior_deviation.reshape(MEMBER_NUMBER, HEIGHT_LAYERS, NCB, CBW).astype(jnp.float32)
    mixed = jnp.einsum('ilbc,bij->jlbc', pieces, weights.astype(jnp.float32))
    return (prior_average + mixed.reshape(MEMBER_NUMBER, HEIGHT_LAYERS, GRID_POINTS)).astype(jnp.bfloat16)
```

```python
import functools

import jax
import jax.numpy as jnp
from jax import lax
from jax.experimental import pallas as pl
from jax.experimental.pallas import tpu as pltpu
from jax.sharding import PartitionSpec as P

NSTEPS = 3
CHUNKS = 4
ROWS = 16


def side_pairs(tiles, mems, step):
    pairs = []
    for mem in range(mems):
        for tile in range(tiles):
            source = tile + step
            if 0 <= source < tiles:
                crossed = (min(tile, source) % 2) == 1
                source_mem = mems - 1 - mem if crossed else mem
                pairs.append((source_mem * tiles + source, mem * tiles + tile))
    return pairs


def gather_body(lists, meta, low, own, high, *refs, for_self, chunks, blocks_dev, width):
    outs = refs[:chunks]
    sems = refs[chunks]
    nloc, count = lists.shape
    half = count // 2
    mem, tile = meta[0], meta[1]
    base = (tile - 1) * blocks_dev
    owner = mem if for_self else 1 - mem
    per_chunk = half // chunks
    for chunk in range(chunks):
        out = outs[chunk]
        for block in range(per_chunk):
            row = owner * half + chunk * per_chunk + block
            for n in range(nloc):
                local = lists[n, row] - base
                which = lax.div(local, blocks_dev)
                start = pl.multiple_of((local - which * blocks_dev) * width, width)
                target = out.at[:, pl.ds((block * nloc + n) * width, width)]
                for index, source in enumerate((low, own, high)):

                    @pl.when(which == index)
                    def _(source=source):
                        pltpu.make_async_copy(
                            source.at[:, pl.ds(start, width)], target, sems.at[chunk]
                        ).start()

    for chunk in range(chunks):
        size = outs[chunk].shape[1]
        pltpu.make_async_copy(own.at[:, pl.ds(0, size)], outs[chunk], sems.at[chunk]).wait()


def gather_blocks(lists, meta, low, own, high, for_self, blocks_dev, width):
    nloc, count = lists.shape
    members = own.shape[0]
    size = (count // 2 // CHUNKS) * nloc * width
    whole = pl.BlockSpec((members, size), lambda i, *_: (0, 0))
    return pl.pallas_call(
        functools.partial(
            gather_body, for_self=for_self, chunks=CHUNKS, blocks_dev=blocks_dev, width=width
        ),
        grid_spec=pltpu.PrefetchScalarGridSpec(
            num_scalar_prefetch=2,
            grid=(1,),
            in_specs=[pl.BlockSpec(memory_space=pl.ANY)] * 3,
            out_specs=[whole] * CHUNKS,
            scratch_shapes=[pltpu.SemaphoreType.DMA((CHUNKS,))],
        ),
        out_shape=[jax.ShapeDtypeStruct((members, size), own.dtype)] * CHUNKS,
        cost_estimate=pl.CostEstimate(
            flops=0, bytes_accessed=4 * CHUNKS * members * size, transcendentals=0
        ),
        name="gather_self" if for_self else "gather_send",
    )(lists, meta, low, own, high)


def split(value):
    high = value.astype(jnp.bfloat16)
    return high, (value - high.astype(jnp.float32)).astype(jnp.bfloat16)


def dot(left, right):
    return lax.dot_general(
        left, right, (((1,), (0,)), ((), ())), preferred_element_type=jnp.float32
    )


def dot3(left, right):
    lh, ll = left
    rh, rl = right
    return dot(lh, rh) + (dot(lh, rl) + dot(ll, rh))


def analysis_body(
    lists, meta, mine, theirs, held, received, low, own, high, *refs, chunk, blocks_dev, width
):
    kept, sent, table, ybuf, sbuf, xbuf, mbuf = refs[-7:]
    nloc, count = lists.shape
    half = count // 2
    mem, tile = meta[0], meta[1]
    parity = lax.rem(tile, 2)
    base = (tile - 1) * blocks_dev
    block = pl.program_id(0)
    row = mem * half + chunk * (half // CHUNKS) + block
    rows = held.shape[0]
    members = 2 * rows
    side = table.shape[0] // 3

    @pl.when(block == 0)
    def _():
        for index, source in enumerate((low, own, high)):
            table[pl.ds(index * side, side), :] = source[...]
        ybuf[pl.ds(members, ROWS), :] = jnp.zeros((ROWS, nloc * width), jnp.bfloat16)

    for n in range(nloc):
        local = lists[n, row] - base
        which = lax.div(local, blocks_dev)
        entry = which * side + (local - which * blocks_dev)
        crossed = ((which == 0) & (parity == 0)) | ((which == 2) & (parity == 1))
        at = pl.ds(n * width, width)
        first = held[:, at].astype(jnp.float32)
        second = received[:, at].astype(jnp.float32)
        mean = (
            jnp.sum(first, axis=0, keepdims=True) + jnp.sum(second, axis=0, keepdims=True)
        ) / members
        value = table[pl.ds(entry, 1), :]
        weight = table[pl.ds(entry + blocks_dev, 1), :]
        innov = value - mean
        d0 = innov.astype(jnp.bfloat16)
        rest = innov - d0.astype(jnp.float32)
        d1, d2 = split(rest)
        ybuf[pl.ds(members, ROWS), at] = jnp.concatenate(
            [d0, d1, d2, jnp.zeros((ROWS - 3, width), jnp.bfloat16)], axis=0
        )
        pert1 = (first - mean).astype(jnp.bfloat16)
        pert2 = (second - mean).astype(jnp.bfloat16)
        scaled1 = (pert1.astype(jnp.float32) * weight).astype(jnp.bfloat16)
        scaled2 = (pert2.astype(jnp.float32) * weight).astype(jnp.bfloat16)
        place1 = pl.multiple_of(jnp.where(crossed, rows, 0), rows)
        place2 = pl.multiple_of(jnp.where(crossed, 0, rows), rows)
        ybuf[pl.ds(place1, rows), at] = pert1
        ybuf[pl.ds(place2, rows), at] = pert2
        sbuf[pl.ds(place1, rows), at] = scaled1
        sbuf[pl.ds(place2, rows), at] = scaled2

    gram = lax.dot_general(
        ybuf[...], sbuf[...], (((1,), (1,)), ((), ())), preferred_element_type=jnp.float32
    )
    matrix = gram[:members]
    rhs = jnp.sum(gram[members:], axis=0, keepdims=True)
    diagonal = lax.broadcasted_iota(jnp.int32, (members, members), 0) == lax.broadcasted_iota(
        jnp.int32, (members, members), 1
    )
    matrix = matrix + jnp.where(diagonal, members - 1.0, 0.0)
    trace = jnp.sum(
        jnp.sum(jnp.where(diagonal, matrix, 0.0), axis=0, keepdims=True), axis=1, keepdims=True
    )
    scale = trace / members
    iterate = matrix / scale
    eye15 = jnp.where(diagonal, 1.5, 0.0)
    inverse_root = eye15 - 0.5 * iterate
    factor = split(inverse_root)
    iterate = dot3(factor, split(iterate))
    for step in range(1, NSTEPS):
        root_parts = split(inverse_root)
        iterate_parts = split(iterate)
        factor = split(eye15 - 0.5 * dot3(iterate_parts, root_parts))
        if step + 1 < NSTEPS:
            iterate = dot3(factor, iterate_parts)
        inverse_root = dot3(root_parts, factor)
    root_parts = split(inverse_root)
    shift = jnp.broadcast_to(rhs, (ROWS, members))
    shift = dot3(split(shift), root_parts)
    shift = dot3(split(shift), root_parts)[:1] / scale
    trans = (jnp.sqrt((members - 1.0) / scale) * inverse_root + shift).astype(jnp.bfloat16)

    layers = mine.shape[0]
    for layer in range(layers):
        at = pl.ds(layer * width, width)
        first = mine[layer].astype(jnp.float32)
        second = theirs[layer].astype(jnp.float32)
        mean = (
            jnp.sum(first, axis=0, keepdims=True) + jnp.sum(second, axis=0, keepdims=True)
        ) / members
        mbuf[:, at] = mean
        xbuf[pl.ds(0, rows), at] = (first - mean).astype(jnp.bfloat16)
        xbuf[pl.ds(rows, rows), at] = (second - mean).astype(jnp.bfloat16)
    result = (dot(trans, xbuf[...]) + mbuf[...]).astype(jnp.bfloat16)
    for layer in range(layers):
        at = slice(layer * width, (layer + 1) * width)
        kept[layer] = result[:rows, at]
        sent[layer] = result[rows:, at]


def analyse(
    lists, meta, mine, theirs, held, received, tables, output, chunk, blocks_dev, width
):
    nloc, count = lists.shape
    half = count // 2
    per_chunk = half // CHUNKS
    layers, rows, cols = mine.shape
    members = 2 * rows
    flops = 2 * per_chunk * members * members * (nloc * width + 18 * members + layers * width)
    span = nloc * width

    def mine_at(i, lists, meta):
        return (0, 0, meta[0] * half + chunk * per_chunk + i)

    tile_block = (layers, rows, width)
    table_spec = pl.BlockSpec(tables[0].shape, lambda i, *_: (0, 0))
    in_specs = [
        pl.BlockSpec(tile_block, mine_at),
        pl.BlockSpec(tile_block, lambda i, *_: (0, 0, chunk * per_chunk + i)),
        pl.BlockSpec((rows, span), lambda i, *_: (0, i)),
        pl.BlockSpec((rows, span), lambda i, *_: (0, i)),
        table_spec,
        table_spec,
        table_spec,
    ]
    operands = [mine, theirs, held, received, *tables]
    aliases = {}
    if output is not None:
        in_specs.append(pl.BlockSpec(memory_space=pl.ANY))
        aliases = {2 + len(operands): 0}
        operands.append(output)
    return pl.pallas_call(
        functools.partial(analysis_body, chunk=chunk, blocks_dev=blocks_dev, width=width),
        grid_spec=pltpu.PrefetchScalarGridSpec(
            num_scalar_prefetch=2,
            grid=(per_chunk,),
            in_specs=in_specs,
            out_specs=[
                pl.BlockSpec(tile_block, mine_at),
                pl.BlockSpec(tile_block, lambda i, *_: (0, 0, i)),
            ],
            scratch_shapes=[
                pltpu.VMEM((3 * tables[0].shape[0], width), jnp.float32),
                pltpu.VMEM((members + ROWS, span), jnp.bfloat16),
                pltpu.VMEM((members, span), jnp.bfloat16),
                pltpu.VMEM((members, layers * width), jnp.bfloat16),
                pltpu.VMEM((1, layers * width), jnp.float32),
            ],
        ),
        out_shape=[
            jax.ShapeDtypeStruct(mine.shape, jnp.bfloat16),
            jax.ShapeDtypeStruct((layers, rows, per_chunk * width), jnp.bfloat16),
        ],
        input_output_aliases=aliases,
        cost_estimate=pl.CostEstimate(
            flops=flops, bytes_accessed=per_chunk * 2 * rows * 2 * (span + 2 * layers * width),
            transcendentals=0,
        ),
        name="analyse",
    )(lists, meta, *operands)


def place_body(meta, piece, output, placed):
    placed[...] = piece[...]


def place(meta, piece, output, chunk):
    layers, rows, cols = piece.shape
    half_chunks = output.shape[2] // 2 // cols

    def place_at(i, meta):
        return (i, 0, (1 - meta[0]) * half_chunks + chunk)

    step = 5 if layers % 5 == 0 else 1
    return pl.pallas_call(
        place_body,
        grid_spec=pltpu.PrefetchScalarGridSpec(
            num_scalar_prefetch=1,
            grid=(layers // step,),
            in_specs=[
                pl.BlockSpec((step, rows, cols), lambda i, *_: (i, 0, 0)),
                pl.BlockSpec(memory_space=pl.ANY),
            ],
            out_specs=pl.BlockSpec((step, rows, cols), place_at),
        ),
        out_shape=jax.ShapeDtypeStruct(output.shape, output.dtype),
        input_output_aliases={2: 0},
        cost_estimate=pl.CostEstimate(
            flops=0, bytes_accessed=4 * layers * rows * cols, transcendentals=0
        ),
        name="place",
    )(meta, piece, output)


def per_device(
    prior_members,
    members_in_reading_space,
    measured_values,
    obs_precision_weights,
    valid_reading_numbers,
    neighbour_lists,
):
    tile_no = lax.axis_index("tile")
    member_no = lax.axis_index("mem")
    tiles = lax.axis_size("tile")
    mems = lax.axis_size("mem")
    both = ("mem", "tile")
    swap = [(0, 1), (1, 0)]
    from_low = side_pairs(tiles, mems, -1)
    from_high = side_pairs(tiles, mems, 1)
    blocks_dev = valid_reading_numbers.shape[0]
    width = members_in_reading_space.shape[1] // blocks_dev
    cols = prior_members.shape[2]

    mine = jnp.transpose(prior_members, (1, 0, 2))
    lists = neighbour_lists.T
    meta = jnp.stack([member_no, tile_no]).astype(jnp.int32)

    own = members_in_reading_space
    low = lax.ppermute(own, both, from_low)
    high = lax.ppermute(own, both, from_high)
    slots = jnp.arange(width, dtype=jnp.int32)
    valid = slots[None, :] < valid_reading_numbers[:, None]
    weight = jnp.where(valid, obs_precision_weights.reshape(blocks_dev, width), 0.0)
    table = jnp.concatenate([measured_values.reshape(blocks_dev, width), weight], axis=0)
    tables = (
        lax.ppermute(table, both, from_low),
        table,
        lax.ppermute(table, both, from_high),
    )
    outgoing = lax.dynamic_slice_in_dim(mine, (1 - member_no) * (cols // 2), cols // 2, 2)
    theirs = lax.ppermute(outgoing, "mem", swap)

    to_send = gather_blocks(lists, meta, low, own, high, False, blocks_dev, width)
    received = [lax.ppermute(piece, "mem", swap) for piece in to_send]
    held = gather_blocks(lists, meta, low, own, high, True, blocks_dev, width)
    output = None
    arrived = []
    for chunk in range(CHUNKS):
        output, sent = analyse(
            lists, meta, mine, theirs, held[chunk], received[chunk], tables, output, chunk,
            blocks_dev, width,
        )
        arrived.append(lax.ppermute(sent, "mem", swap))
    for chunk in range(CHUNKS):
        output = place(meta, arrived[chunk], output, chunk)
    return jnp.transpose(output, (1, 0, 2))


def solution(mesh):
    in_specs = (
        P("mem", None, "tile"),
        P("mem", "tile"),
        P("tile"),
        P("tile"),
        P("tile"),
        P("tile", None),
    )
    out_specs = P("mem", None, "tile")
    return jax.shard_map(
        per_device, mesh=mesh, in_specs=in_specs, out_specs=out_specs, check_vma=False
    )
```

```python
import functools

import jax
import jax.numpy as jnp
from jax import lax
from jax.experimental import pallas as pl
from jax.experimental.pallas import tpu as pltpu
from jax.sharding import PartitionSpec as P


NSTEPS = 3
CHUNKS = 4
ROWS = 16


def side_pairs(tiles, mems, step):
    pairs = []
    for mem in range(mems):
        for tile in range(tiles):
            source = tile + step
            if 0 <= source < tiles:
                crossed = (min(tile, source) % 2) == 1
                source_mem = mems - 1 - mem if crossed else mem
                pairs.append((source_mem * tiles + source, mem * tiles + tile))
    return pairs


def gather_body(lists, meta, low, own, high, *refs, for_self, chunks, blocks_dev, width):
    outs = refs[:chunks]
    sems = refs[chunks]
    nloc, count = lists.shape
    half = count // 2
    mem, tile = meta[0], meta[1]
    base = (tile - 1) * blocks_dev
    owner = mem if for_self else 1 - mem
    per_chunk = half // chunks
    for chunk in range(chunks):
        out = outs[chunk]
        for block in range(per_chunk):
            row = owner * half + chunk * per_chunk + block
            for n in range(nloc):
                local = lists[n, row] - base
                which = lax.div(local, blocks_dev)
                start = pl.multiple_of((local - which * blocks_dev) * width, width)
                target = out.at[:, pl.ds((block * nloc + n) * width, width)]
                for index, source in enumerate((low, own, high)):

                    @pl.when(which == index)
                    def _(source=source):
                        pltpu.make_async_copy(
                            source.at[:, pl.ds(start, width)], target, sems.at[chunk]
                        ).start()

    for chunk in range(chunks):
        size = outs[chunk].shape[1]
        pltpu.make_async_copy(own.at[:, pl.ds(0, size)], outs[chunk], sems.at[chunk]).wait()


def gather_blocks(lists, meta, low, own, high, for_self, blocks_dev, width):
    nloc, count = lists.shape
    members = own.shape[0]
    size = (count // 2 // CHUNKS) * nloc * width
    whole = pl.BlockSpec((members, size), lambda i, *_: (0, 0))
    return pl.pallas_call(
        functools.partial(
            gather_body, for_self=for_self, chunks=CHUNKS, blocks_dev=blocks_dev, width=width
        ),
        grid_spec=pltpu.PrefetchScalarGridSpec(
            num_scalar_prefetch=2,
            grid=(1,),
            in_specs=[pl.BlockSpec(memory_space=pltpu.HBM)] * 3,
            out_specs=[whole] * CHUNKS,
            scratch_shapes=[pltpu.SemaphoreType.DMA((CHUNKS,))],
        ),
        out_shape=[jax.ShapeDtypeStruct((members, size), own.dtype)] * CHUNKS,
        cost_estimate=pl.CostEstimate(
            flops=0, bytes_accessed=4 * CHUNKS * members * size, transcendentals=0
        ),
        compiler_params=pltpu.CompilerParams(vmem_limit_bytes=8 << 20),
        name="gather_self" if for_self else "gather_send",
    )(lists, meta, low, own, high)


def split(value):
    high = value.astype(jnp.bfloat16)
    return high, (value - high.astype(jnp.float32)).astype(jnp.bfloat16)


def dot(left, right):
    return lax.dot_general(
        left, right, (((1,), (0,)), ((), ())), preferred_element_type=jnp.float32
    )


def dot3(left, right):
    lh, ll = left
    rh, rl = right
    return dot(lh, rh) + (dot(lh, rl) + dot(ll, rh))


def analysis_body(
    lists, meta, mine, theirs, held, received, low, own, high, *refs, chunk, blocks_dev, width
):
    kept, sent, table, ybuf, sbuf, xbuf, mbuf = refs[-7:]
    nloc, count = lists.shape
    half = count // 2
    mem, tile = meta[0], meta[1]
    parity = lax.rem(tile, 2)
    base = (tile - 1) * blocks_dev
    block = pl.program_id(0)
    row = mem * half + chunk * (half // CHUNKS) + block
    rows = held.shape[0]
    members = 2 * rows
    side = table.shape[0] // 3

    @pl.when(block == 0)
    def _():
        for index, source in enumerate((low, own, high)):
            table[pl.ds(index * side, side), :] = source[...]
        ybuf[pl.ds(members, ROWS), :] = jnp.zeros((ROWS, nloc * width), jnp.bfloat16)

    for n in range(nloc):
        local = lists[n, row] - base
        which = lax.div(local, blocks_dev)
        entry = which * side + (local - which * blocks_dev)
        crossed = ((which == 0) & (parity == 0)) | ((which == 2) & (parity == 1))
        at = pl.ds(n * width, width)
        first = held[:, at].astype(jnp.float32)
        second = received[:, at].astype(jnp.float32)
        mean = (
            jnp.sum(first, axis=0, keepdims=True) + jnp.sum(second, axis=0, keepdims=True)
        ) / members
        value = table[pl.ds(entry, 1), :]
        weight = table[pl.ds(entry + blocks_dev, 1), :]
        innov = value - mean
        d0 = innov.astype(jnp.bfloat16)
        rest = innov - d0.astype(jnp.float32)
        d1, d2 = split(rest)
        ybuf[pl.ds(members, ROWS), at] = jnp.concatenate(
            [d0, d1, d2, jnp.zeros((ROWS - 3, width), jnp.bfloat16)], axis=0
        )
        pert1 = (first - mean).astype(jnp.bfloat16)
        pert2 = (second - mean).astype(jnp.bfloat16)
        scaled1 = (pert1.astype(jnp.float32) * weight).astype(jnp.bfloat16)
        scaled2 = (pert2.astype(jnp.float32) * weight).astype(jnp.bfloat16)
        place1 = pl.multiple_of(jnp.where(crossed, rows, 0), rows)
        place2 = pl.multiple_of(jnp.where(crossed, 0, rows), rows)
        ybuf[pl.ds(place1, rows), at] = pert1
        ybuf[pl.ds(place2, rows), at] = pert2
        sbuf[pl.ds(place1, rows), at] = scaled1
        sbuf[pl.ds(place2, rows), at] = scaled2

    gram = lax.dot_general(
        ybuf[...], sbuf[...], (((1,), (1,)), ((), ())), preferred_element_type=jnp.float32
    )
    matrix = gram[:members]
    rhs = jnp.sum(gram[members:], axis=0, keepdims=True)
    diagonal = lax.broadcasted_iota(jnp.int32, (members, members), 0) == lax.broadcasted_iota(
        jnp.int32, (members, members), 1
    )
    matrix = matrix + jnp.where(diagonal, members - 1.0, 0.0)
    trace = jnp.sum(
        jnp.sum(jnp.where(diagonal, matrix, 0.0), axis=0, keepdims=True), axis=1, keepdims=True
    )
    scale = trace / members
    iterate = matrix / scale
    eye15 = jnp.where(diagonal, 1.5, 0.0)
    inverse_root = eye15 - 0.5 * iterate
    factor = split(inverse_root)
    iterate = dot3(factor, split(iterate))
    for step in range(1, NSTEPS):
        root_parts = split(inverse_root)
        iterate_parts = split(iterate)
        factor = split(eye15 - 0.5 * dot3(iterate_parts, root_parts))
        if step + 1 < NSTEPS:
            iterate = dot3(factor, iterate_parts)
        inverse_root = dot3(root_parts, factor)
    root_parts = split(inverse_root)
    shift = jnp.broadcast_to(rhs, (ROWS, members))
    shift = dot3(split(shift), root_parts)
    shift = dot3(split(shift), root_parts)[:1] / scale
    trans = (jnp.sqrt((members - 1.0) / scale) * inverse_root + shift).astype(jnp.bfloat16)

    layers = mine.shape[0]
    for layer in range(layers):
        at = pl.ds(layer * width, width)
        first = mine[layer].astype(jnp.float32)
        second = theirs[layer].astype(jnp.float32)
        mean = (
            jnp.sum(first, axis=0, keepdims=True) + jnp.sum(second, axis=0, keepdims=True)
        ) / members
        mbuf[:, at] = mean
        xbuf[pl.ds(0, rows), at] = (first - mean).astype(jnp.bfloat16)
        xbuf[pl.ds(rows, rows), at] = (second - mean).astype(jnp.bfloat16)
    result = (dot(trans, xbuf[...]) + mbuf[...]).astype(jnp.bfloat16)
    for layer in range(layers):
        at = slice(layer * width, (layer + 1) * width)
        kept[layer] = result[:rows, at]
        sent[layer] = result[rows:, at]


def analyse(
    lists, meta, mine, theirs, held, received, tables, output, chunk, skipped, blocks_dev, width
):
    nloc, count = lists.shape
    half = count // 2
    per_chunk = half // CHUNKS
    layers, rows, _ = mine.shape
    members = 2 * rows
    flops = 2 * per_chunk * members * members * (nloc * width + 18 * members + layers * width)
    span = nloc * width

    def mine_at(i, lists, meta):
        return (0, 0, meta[0] * half + chunk * per_chunk + i)

    tile_block = (layers, rows, width)
    table_spec = pl.BlockSpec(tables[0].shape, lambda i, *_: (0, 0))
    in_specs = [
        pl.BlockSpec(tile_block, mine_at),
        pl.BlockSpec(tile_block, lambda i, *_: (0, 0, (chunk - skipped) * per_chunk + i)),
        pl.BlockSpec((rows, span), lambda i, *_: (0, i)),
        pl.BlockSpec((rows, span), lambda i, *_: (0, i)),
        table_spec,
        table_spec,
        table_spec,
    ]
    operands = [mine, theirs, held, received, *tables]
    aliases = {}
    if output is not None:
        in_specs.append(pl.BlockSpec(memory_space=pl.ANY))
        aliases = {2 + len(operands): 0}
        operands.append(output)
    return pl.pallas_call(
        functools.partial(analysis_body, chunk=chunk, blocks_dev=blocks_dev, width=width),
        grid_spec=pltpu.PrefetchScalarGridSpec(
            num_scalar_prefetch=2,
            grid=(per_chunk,),
            in_specs=in_specs,
            out_specs=[
                pl.BlockSpec(tile_block, mine_at),
                pl.BlockSpec(tile_block, lambda i, *_: (0, 0, i)),
            ],
            scratch_shapes=[
                pltpu.VMEM((3 * tables[0].shape[0], width), jnp.float32),
                pltpu.VMEM((members + ROWS, span), jnp.bfloat16),
                pltpu.VMEM((members, span), jnp.bfloat16),
                pltpu.VMEM((members, layers * width), jnp.bfloat16),
                pltpu.VMEM((1, layers * width), jnp.float32),
            ],
        ),
        out_shape=[
            jax.ShapeDtypeStruct(mine.shape, jnp.bfloat16),
            jax.ShapeDtypeStruct((layers, rows, per_chunk * width), jnp.bfloat16),
        ],
        input_output_aliases=aliases,
        cost_estimate=pl.CostEstimate(
            flops=flops, bytes_accessed=per_chunk * 2 * rows * 2 * (span + 2 * layers * width),
            transcendentals=0,
        ),
        compiler_params=pltpu.CompilerParams(vmem_limit_bytes=24 << 20),
        name="analyse",
    )(lists, meta, *operands)


def place_body(meta, piece, output, placed, sem, *, chunk):
    cols = piece.shape[2]
    start = (1 - meta[0]) * (placed.shape[2] // 2) + chunk * cols
    copy = pltpu.make_async_copy(
        piece, placed.at[:, :, pl.ds(pl.multiple_of(start, cols), cols)], sem
    )
    copy.start()
    copy.wait()


def place(meta, piece, output, chunk):
    return pl.pallas_call(
        functools.partial(place_body, chunk=chunk),
        grid_spec=pltpu.PrefetchScalarGridSpec(
            num_scalar_prefetch=1,
            grid=(1,),
            in_specs=[pl.BlockSpec(memory_space=pl.ANY)] * 2,
            out_specs=pl.BlockSpec(memory_space=pl.ANY),
            scratch_shapes=[pltpu.SemaphoreType.DMA],
        ),
        out_shape=jax.ShapeDtypeStruct(output.shape, output.dtype),
        input_output_aliases={2: 0},
        cost_estimate=pl.CostEstimate(
            flops=0, bytes_accessed=4 * piece.size, transcendentals=0
        ),
        compiler_params=pltpu.CompilerParams(vmem_limit_bytes=2 << 20),
        name="place",
    )(meta, piece, output)


def per_device(
    prior_members,
    members_in_reading_space,
    measured_values,
    obs_precision_weights,
    valid_reading_numbers,
    neighbour_lists,
):
    tile_no = lax.axis_index("tile")
    member_no = lax.axis_index("mem")
    tiles = lax.axis_size("tile")
    mems = lax.axis_size("mem")
    both = ("mem", "tile")
    swap = [(0, 1), (1, 0)]
    from_low = side_pairs(tiles, mems, -1)
    from_high = side_pairs(tiles, mems, 1)
    blocks_dev = valid_reading_numbers.shape[0]
    width = members_in_reading_space.shape[1] // blocks_dev
    cols = prior_members.shape[2]

    mine = jnp.transpose(prior_members, (1, 0, 2))
    lists = neighbour_lists.T
    meta = jnp.stack([member_no, tile_no]).astype(jnp.int32)

    own = members_in_reading_space
    half = cols // 2
    piece = half // CHUNKS
    prior = []
    for start, size in ((0, piece), (piece, half - piece)):
        outgoing = lax.dynamic_slice_in_dim(mine, (1 - member_no) * half + start, size, 2)
        prior.append(lax.ppermute(outgoing, "mem", swap))
    low = lax.ppermute(own, both, from_low)
    high = lax.ppermute(own, both, from_high)
    slots = jnp.arange(width, dtype=jnp.int32)
    valid = slots[None, :] < valid_reading_numbers[:, None]
    weight = jnp.where(valid, obs_precision_weights.reshape(blocks_dev, width), 0.0)
    table = jnp.concatenate([measured_values.reshape(blocks_dev, width), weight], axis=0)
    table_low = lax.ppermute(table, both, from_low)
    table_high = lax.ppermute(table, both, from_high)
    tables = (table_low, table, table_high)

    to_send = gather_blocks(lists, meta, low, own, high, False, blocks_dev, width)
    received = []
    for chunk in range(CHUNKS):
        received.append(lax.ppermute(to_send[chunk], "mem", swap))
    held = gather_blocks(lists, meta, low, own, high, True, blocks_dev, width)
    output = None
    arrived = []
    for chunk in range(CHUNKS):
        output, sent = analyse(
            lists, meta, mine, prior[min(chunk, 1)], held[chunk], received[chunk], tables,
            output, chunk, min(chunk, 1), blocks_dev, width,
        )
        arrived.append(lax.ppermute(sent, "mem", swap))
    for chunk in range(CHUNKS):
        output = place(meta, arrived[chunk], output, chunk)
    return jnp.transpose(output, (1, 0, 2))


def solution(mesh):
    in_specs = (
        P("mem", None, "tile"),
        P("mem", "tile"),
        P("tile"),
        P("tile"),
        P("tile"),
        P("tile", None),
    )
    out_specs = P("mem", None, "tile")

    return jax.shard_map(
        per_device, mesh=mesh, in_specs=in_specs, out_specs=out_specs, check_vma=False
    )
```

```python
import functools

import jax
import jax.numpy as jnp
from jax import lax
from jax.experimental import pallas as pl
from jax.experimental.pallas import tpu as pltpu
from jax.sharding import PartitionSpec as P


NSTEPS = 3
CHUNKS = 4
ROWS = 16


def side_pairs(tiles, mems, step):
    pairs = []
    for mem in range(mems):
        for tile in range(tiles):
            source = tile + step
            if 0 <= source < tiles:
                crossed = (min(tile, source) % 2) == 1
                source_mem = mems - 1 - mem if crossed else mem
                pairs.append((source_mem * tiles + source, mem * tiles + tile))
    return pairs


def locate(lists, meta, row, n, blocks_dev):
    mem, tile = meta[0], meta[1]
    parity = lax.rem(tile, 2)
    local = lists[n, row] - (tile - 1) * blocks_dev
    which = lax.div(local, blocks_dev)
    inside = local - which * blocks_dev
    crossed = ((which == 0) & (parity == 0)) | ((which == 2) & (parity == 1))
    source = jnp.where(crossed, 1 - mem, mem)
    part = lax.div(inside, blocks_dev // 2)
    return which, inside, source, part == source, inside - part * (blocks_dev // 2)


def gather_body(lists, meta, *refs, for_self, chunks, blocks_dev, width):
    tiles = [(refs[2 * k], refs[2 * k + 1]) for k in range(3)]
    outs = refs[6 : 6 + chunks]
    sem = refs[6 + chunks]
    nloc, count = lists.shape
    half = count // 2
    owner = meta[0] if for_self else 1 - meta[0]
    per_chunk = half // chunks
    rows = tiles[0][0].shape[0]

    for chunk in range(chunks):
        out = outs[chunk]

        @pl.loop(0, per_chunk * nloc)
        def _(slot, chunk=chunk, out=out):
            block = lax.div(slot, nloc)
            n = slot - block * nloc
            row = owner * half + chunk * per_chunk + block
            which, _, source, here, index = locate(lists, meta, row, n, blocks_dev)
            start = pl.multiple_of(index * width, width)
            at = pl.ds(pl.multiple_of(slot * width, width), width)
            first = pl.multiple_of(jnp.where(source == owner, 0, rows), rows)
            second = pl.multiple_of(jnp.where(source == owner, rows, 0), rows)
            for k, (own_part, other_part) in enumerate(tiles):

                @pl.when(here & (which == k))
                def _(own_part=own_part, other_part=other_part):
                    pltpu.make_async_copy(
                        own_part.at[:, pl.ds(start, width)], out.at[pl.ds(first, rows), at], sem
                    ).start()
                    pltpu.make_async_copy(
                        other_part.at[:, pl.ds(start, width)], out.at[pl.ds(second, rows), at], sem
                    ).start()

    for chunk in range(chunks):
        out = outs[chunk]

        @pl.loop(0, per_chunk * nloc)
        def _(slot, chunk=chunk, out=out):
            block = lax.div(slot, nloc)
            row = owner * half + chunk * per_chunk + block
            _, _, _, here, _ = locate(lists, meta, row, slot - block * nloc, blocks_dev)

            @pl.when(here)
            def _():
                whole = out.at[:, pl.ds(0, width)]
                pltpu.make_async_copy(whole, whole, sem).wait()


def gather_blocks(lists, meta, tiles, for_self, chunks, blocks_dev, width):
    nloc, count = lists.shape
    members = 2 * tiles[0].shape[0]
    size = (count // 2 // chunks) * nloc * width
    whole = pl.BlockSpec((members, size), lambda i, *_: (0, 0))
    return pl.pallas_call(
        functools.partial(
            gather_body, for_self=for_self, chunks=chunks, blocks_dev=blocks_dev, width=width
        ),
        grid_spec=pltpu.PrefetchScalarGridSpec(
            num_scalar_prefetch=2,
            grid=(1,),
            in_specs=[pl.BlockSpec(memory_space=pl.ANY)] * 6,
            out_specs=[whole] * chunks,
            scratch_shapes=[pltpu.SemaphoreType.DMA],
        ),
        out_shape=[jax.ShapeDtypeStruct((members, size), tiles[0].dtype)] * chunks,
        cost_estimate=pl.CostEstimate(
            flops=0, bytes_accessed=2 * chunks * members * size, transcendentals=0
        ),
        compiler_params=pltpu.CompilerParams(vmem_limit_bytes=12 << 20),
        name="gather_self" if for_self else "gather_send",
    )(lists, meta, *tiles)


def split(value):
    high = value.astype(jnp.bfloat16)
    return high, (value - high.astype(jnp.float32)).astype(jnp.bfloat16)


def dot(left, right):
    return lax.dot_general(
        left, right, (((1,), (0,)), ((), ())), preferred_element_type=jnp.float32
    )


def dot3(left, right):
    lh, ll = left
    rh, rl = right
    return dot(lh, rh) + (dot(lh, rl) + dot(ll, rh))


def parts3(value):
    high = value.astype(jnp.bfloat16)
    mid, low = split(value - high.astype(jnp.float32))
    return [high, mid, low]


def local_gram(lists, meta, row, held, low, own, high, ybuf, sbuf, blocks_dev, width):
    nloc = lists.shape[0]
    members = held.shape[0]
    for n in range(nloc):
        which, inside, _, here, _ = locate(lists, meta, row, n, blocks_dev)
        at = pl.ds(n * width, width)

        @pl.when(jnp.logical_not(here))
        def _(at=at):
            ybuf[:, at] = jnp.zeros((members + ROWS, width), jnp.bfloat16)
            sbuf[:, at] = jnp.zeros((members, width), jnp.bfloat16)

        @pl.when(here)
        def _(at=at, which=which, inside=inside):
            raw = held[:, at].astype(jnp.float32)
            mean = jnp.sum(raw, axis=0, keepdims=True) / members

            def entry(index):
                at_low = low[pl.ds(index, 1), :]
                at_own = own[pl.ds(index, 1), :]
                at_high = high[pl.ds(index, 1), :]
                return jnp.where(which == 0, at_low, jnp.where(which == 1, at_own, at_high))

            value = entry(inside)
            weight = entry(inside + blocks_dev)
            ybuf[pl.ds(members, ROWS), at] = jnp.concatenate(
                [*parts3(value - mean), jnp.zeros((ROWS - 3, width), jnp.bfloat16)], axis=0
            )
            pert = (raw - mean).astype(jnp.bfloat16)
            ybuf[pl.ds(0, members), at] = pert
            sbuf[:, at] = (pert.astype(jnp.float32) * weight).astype(jnp.bfloat16)

    gram = lax.dot_general(
        ybuf[...], sbuf[...], (((1,), (1,)), ((), ())), preferred_element_type=jnp.float32
    )
    return gram[:members], jnp.sum(gram[members:], axis=0, keepdims=True)


def on_diagonal(size):
    return lax.broadcasted_iota(jnp.int32, (size, size), 0) == lax.broadcasted_iota(
        jnp.int32, (size, size), 1
    )


def partial_body(lists, meta, held, low, own, high, *refs, blocks_dev, width):
    outs, ybuf, sbuf = refs[:CHUNKS], refs[CHUNKS], refs[CHUNKS + 1]
    half = lists.shape[1] // 2
    block = pl.program_id(0)
    matrix, rhs = local_gram(
        lists, meta, (1 - meta[0]) * half + block, held, low, own, high, ybuf, sbuf,
        blocks_dev, width,
    )
    members = matrix.shape[0]
    q = members // 4
    diagonal = jnp.sum(jnp.where(on_diagonal(members), matrix, 0.0), axis=0, keepdims=True)
    lane = lax.broadcasted_iota(jnp.int32, (q, members), 1)
    second = jnp.where(lane < q, pltpu.roll(matrix[3 * q :], q, 1), matrix[q : 2 * q])
    third = jnp.concatenate(
        [matrix[2 * q + q // 2 : 3 * q, 2 * q :], matrix[2 * q : 2 * q + q // 2, 2 * q :]], axis=1
    )
    extra = jnp.concatenate(
        [*parts3(rhs), *parts3(diagonal), jnp.zeros((ROWS - 6, members), jnp.bfloat16)], axis=0
    )
    per_chunk = half // CHUNKS
    for chunk in range(CHUNKS):

        @pl.when((block >= chunk * per_chunk) & (block < (chunk + 1) * per_chunk))
        def _(out=outs[chunk]):
            out[0, pl.ds(0, q), :] = matrix[:q].astype(jnp.bfloat16)
            out[0, pl.ds(q, q), :] = second.astype(jnp.bfloat16)
            out[0, pl.ds(2 * q, q // 2), :] = third.astype(jnp.bfloat16)
            out[0, pl.ds(2 * q + q // 2, ROWS), :] = extra


def partial_sums(lists, meta, held, tables, blocks_dev, width):
    nloc, count = lists.shape
    half = count // 2
    per_chunk = half // CHUNKS
    members = held.shape[0]
    span = nloc * width
    packed = (1, members // 2 + members // 8 + ROWS, members)
    table_spec = pl.BlockSpec(tables[0].shape, lambda i, *_: (0, 0))

    def out_spec(chunk):
        return pl.BlockSpec(
            packed, lambda i, *_: (jnp.clip(i - chunk * per_chunk, 0, per_chunk - 1), 0, 0)
        )

    return pl.pallas_call(
        functools.partial(partial_body, blocks_dev=blocks_dev, width=width),
        grid_spec=pltpu.PrefetchScalarGridSpec(
            num_scalar_prefetch=2,
            grid=(half,),
            in_specs=[pl.BlockSpec((members, span), lambda i, *_: (0, i))] + [table_spec] * 3,
            out_specs=[out_spec(chunk) for chunk in range(CHUNKS)],
            scratch_shapes=[
                pltpu.VMEM((members + ROWS, span), jnp.bfloat16),
                pltpu.VMEM((members, span), jnp.bfloat16),
            ],
        ),
        out_shape=[jax.ShapeDtypeStruct((per_chunk, *packed[1:]), jnp.bfloat16)] * CHUNKS,
        cost_estimate=pl.CostEstimate(
            flops=2 * half * members * members * span,
            bytes_accessed=2 * members * half * span,
            transcendentals=0,
        ),
        compiler_params=pltpu.CompilerParams(vmem_limit_bytes=16 << 20),
        name="partial_sums",
    )(lists, meta, held, *tables)


def analysis_body(
    lists, meta, mine, theirs, held, received, low, own, high, *refs, chunk, blocks_dev, width
):
    kept, sent, ubuf, ybuf, sbuf, xbuf, mbuf = refs[-7:]
    half = lists.shape[1] // 2
    row = meta[0] * half + chunk * (half // CHUNKS) + pl.program_id(0)
    rows = mine.shape[1]
    members = 2 * rows

    matrix, rhs = local_gram(
        lists, meta, row, held, low, own, high, ybuf, sbuf, blocks_dev, width
    )
    q = members // 4
    ubuf[pl.ds(0, q), :] = received[0, pl.ds(0, q), :].astype(jnp.float32)
    second = received[0, pl.ds(q, q), :].astype(jnp.float32)
    ubuf[pl.ds(q, q), :] = second
    third = received[0, pl.ds(2 * q, q // 2), :].astype(jnp.float32)
    ubuf[pl.ds(2 * q, q // 2), pl.ds(2 * q, 2 * q)] = third[:, 2 * q :]
    ubuf[pl.ds(2 * q + q // 2, q // 2), pl.ds(2 * q, 2 * q)] = third[:, : 2 * q]
    ubuf[pl.ds(3 * q, q), :] = pltpu.roll(second, 3 * q, 1)
    extra = received[0, pl.ds(2 * q + q // 2, ROWS), :].astype(jnp.float32)
    rhs = rhs + jnp.sum(extra[:3], axis=0, keepdims=True)
    upper = ubuf[...]
    block_row = lax.div(lax.broadcasted_iota(jnp.int32, (members, members), 0), q)
    block_col = lax.div(lax.broadcasted_iota(jnp.int32, (members, members), 1), q)
    other = jnp.where(block_row <= block_col, upper, upper.T)
    diagonal = on_diagonal(members)
    other = jnp.where(diagonal, jnp.sum(extra[3:6], axis=0, keepdims=True), other)
    matrix = matrix + other
    matrix = matrix + jnp.where(diagonal, members - 1.0, 0.0)
    trace = jnp.sum(
        jnp.sum(jnp.where(diagonal, matrix, 0.0), axis=0, keepdims=True), axis=1, keepdims=True
    )
    scale = trace / members
    iterate = matrix / scale
    eye15 = jnp.where(diagonal, 1.5, 0.0)
    inverse_root = eye15 - 0.5 * iterate
    factor = split(inverse_root)
    iterate = dot3(factor, split(iterate))
    for step in range(1, NSTEPS):
        root_parts = split(inverse_root)
        iterate_parts = split(iterate)
        factor = split(eye15 - 0.5 * dot3(iterate_parts, root_parts))
        if step + 1 < NSTEPS:
            iterate = dot3(factor, iterate_parts)
        inverse_root = dot3(root_parts, factor)
    root_parts = split(inverse_root)
    shift = jnp.broadcast_to(rhs, (ROWS, members))
    shift = dot3(split(shift), root_parts)
    shift = dot3(split(shift), root_parts)[:1] / scale
    trans = (jnp.sqrt((members - 1.0) / scale) * inverse_root + shift).astype(jnp.bfloat16)

    layers = mine.shape[0]
    for layer in range(layers):
        at = pl.ds(layer * width, width)
        first = mine[layer].astype(jnp.float32)
        second = theirs[layer].astype(jnp.float32)
        mean = (
            jnp.sum(first, axis=0, keepdims=True) + jnp.sum(second, axis=0, keepdims=True)
        ) / members
        mbuf[:, at] = mean
        xbuf[pl.ds(0, rows), at] = (first - mean).astype(jnp.bfloat16)
        xbuf[pl.ds(rows, rows), at] = (second - mean).astype(jnp.bfloat16)
    result = (dot(trans, xbuf[...]) + mbuf[...]).astype(jnp.bfloat16)
    for layer in range(layers):
        at = slice(layer * width, (layer + 1) * width)
        kept[layer] = result[:rows, at]
        sent[layer] = result[rows:, at]


def analyse(
    lists, meta, mine, theirs, held, received, tables, output, chunk, blocks_dev, width
):
    nloc, count = lists.shape
    half = count // 2
    per_chunk = half // CHUNKS
    layers, rows, _ = mine.shape
    members = 2 * rows
    flops = 2 * per_chunk * members * members * (nloc * width + 18 * members + layers * width)
    span = nloc * width

    def mine_at(i, lists, meta):
        return (0, 0, meta[0] * half + chunk * per_chunk + i)

    tile_block = (layers, rows, width)
    table_spec = pl.BlockSpec(tables[0].shape, lambda i, *_: (0, 0))
    in_specs = [
        pl.BlockSpec(tile_block, mine_at),
        pl.BlockSpec(tile_block, lambda i, *_: (0, 0, chunk * per_chunk + i)),
        pl.BlockSpec((members, span), lambda i, *_: (0, i)),
        pl.BlockSpec((1, *received.shape[1:]), lambda i, *_: (i, 0, 0)),
        table_spec,
        table_spec,
        table_spec,
    ]
    operands = [mine, theirs, held, received, *tables]
    aliases = {}
    if output is not None:
        in_specs.append(pl.BlockSpec(memory_space=pl.ANY))
        aliases = {2 + len(operands): 0}
        operands.append(output)
    return pl.pallas_call(
        functools.partial(analysis_body, chunk=chunk, blocks_dev=blocks_dev, width=width),
        grid_spec=pltpu.PrefetchScalarGridSpec(
            num_scalar_prefetch=2,
            grid=(per_chunk,),
            in_specs=in_specs,
            out_specs=[
                pl.BlockSpec(tile_block, mine_at),
                pl.BlockSpec(tile_block, lambda i, *_: (0, 0, i)),
            ],
            scratch_shapes=[
                pltpu.VMEM((members, members), jnp.float32),
                pltpu.VMEM((members + ROWS, span), jnp.bfloat16),
                pltpu.VMEM((members, span), jnp.bfloat16),
                pltpu.VMEM((members, layers * width), jnp.bfloat16),
                pltpu.VMEM((1, layers * width), jnp.float32),
            ],
        ),
        out_shape=[
            jax.ShapeDtypeStruct(mine.shape, jnp.bfloat16),
            jax.ShapeDtypeStruct((layers, rows, per_chunk * width), jnp.bfloat16),
        ],
        input_output_aliases=aliases,
        cost_estimate=pl.CostEstimate(
            flops=flops, bytes_accessed=per_chunk * 2 * rows * 2 * (span + 2 * layers * width),
            transcendentals=0,
        ),
        compiler_params=pltpu.CompilerParams(vmem_limit_bytes=24 << 20),
        name="analyse",
    )(lists, meta, *operands)


def place_body(meta, piece, output, placed, sem, *, chunk):
    cols = piece.shape[2]
    start = (1 - meta[0]) * (placed.shape[2] // 2) + chunk * cols
    copy = pltpu.make_async_copy(
        piece, placed.at[:, :, pl.ds(pl.multiple_of(start, cols), cols)], sem
    )
    copy.start()
    copy.wait()


def place(meta, piece, output, chunk):
    return pl.pallas_call(
        functools.partial(place_body, chunk=chunk),
        grid_spec=pltpu.PrefetchScalarGridSpec(
            num_scalar_prefetch=1,
            grid=(1,),
            in_specs=[pl.BlockSpec(memory_space=pl.ANY)] * 2,
            out_specs=pl.BlockSpec(memory_space=pl.ANY),
            scratch_shapes=[pltpu.SemaphoreType.DMA],
        ),
        out_shape=jax.ShapeDtypeStruct(output.shape, output.dtype),
        input_output_aliases={2: 0},
        cost_estimate=pl.CostEstimate(
            flops=0, bytes_accessed=4 * piece.size, transcendentals=0
        ),
        compiler_params=pltpu.CompilerParams(vmem_limit_bytes=2 << 20),
        name="place",
    )(meta, piece, output)


def per_device(
    prior_members,
    members_in_reading_space,
    measured_values,
    obs_precision_weights,
    valid_reading_numbers,
    neighbour_lists,
):
    tile_no = lax.axis_index("tile")
    member_no = lax.axis_index("mem")
    tiles = lax.axis_size("tile")
    mems = lax.axis_size("mem")
    both = ("mem", "tile")
    swap = [(0, 1), (1, 0)]
    from_low = side_pairs(tiles, mems, -1)
    from_high = side_pairs(tiles, mems, 1)
    blocks_dev = valid_reading_numbers.shape[0]
    width = members_in_reading_space.shape[1] // blocks_dev
    cols = prior_members.shape[2]

    mine = jnp.transpose(prior_members, (1, 0, 2))
    lists = neighbour_lists.T
    meta = jnp.stack([member_no, tile_no]).astype(jnp.int32)

    obs = members_in_reading_space
    obs_half = obs.shape[1] // 2
    other_set = lax.dynamic_slice_in_dim(obs, (1 - member_no) * obs_half, obs_half, 1)
    swapped = lax.ppermute(other_set, "mem", swap)
    own_set = lax.dynamic_slice_in_dim(obs, member_no * obs_half, obs_half, 1)
    low_own = lax.ppermute(own_set, both, from_low)
    high_own = lax.ppermute(own_set, both, from_high)
    half = cols // 2
    outgoing = lax.dynamic_slice_in_dim(mine, (1 - member_no) * half, half, 2)
    theirs = lax.ppermute(outgoing, "mem", swap)
    low_other = lax.ppermute(swapped, both, from_low)
    high_other = lax.ppermute(swapped, both, from_high)
    tiles_held = (low_own, low_other, own_set, swapped, high_own, high_other)
    slots = jnp.arange(width, dtype=jnp.int32)
    valid = slots[None, :] < valid_reading_numbers[:, None]
    weight = jnp.where(valid, obs_precision_weights.reshape(blocks_dev, width), 0.0)
    table = jnp.concatenate([measured_values.reshape(blocks_dev, width), weight], axis=0)
    table_low = lax.ppermute(table, both, from_low)
    table_high = lax.ppermute(table, both, from_high)
    tables = (table_low, table, table_high)

    (to_send,) = gather_blocks(lists, meta, tiles_held, False, 1, blocks_dev, width)
    sums = partial_sums(lists, meta, to_send, tables, blocks_dev, width)
    received = []
    for chunk in range(CHUNKS):
        received.append(lax.ppermute(sums[chunk], "mem", swap))
    held = gather_blocks(lists, meta, tiles_held, True, CHUNKS, blocks_dev, width)
    output = None
    arrived = []
    for chunk in range(CHUNKS):
        output, sent = analyse(
            lists, meta, mine, theirs, held[chunk], received[chunk], tables, output, chunk,
            blocks_dev, width,
        )
        arrived.append(lax.ppermute(sent, "mem", swap))
    for chunk in range(CHUNKS):
        output = place(meta, arrived[chunk], output, chunk)
    return jnp.transpose(output, (1, 0, 2))


def solution(mesh):
    in_specs = (
        P("mem", None, "tile"),
        P("mem", "tile"),
        P("tile"),
        P("tile"),
        P("tile"),
        P("tile", None),
    )
    out_specs = P("mem", None, "tile")

    return jax.shard_map(
        per_device, mesh=mesh, in_specs=in_specs, out_specs=out_specs, check_vma=False
    )
```

```python
import functools

import jax
import jax.numpy as jnp
from jax import lax
from jax.experimental import pallas as pl
from jax.experimental.pallas import tpu as pltpu
from jax.sharding import PartitionSpec as P


NSTEPS = 3
ROWS = 16
AHEAD = 3
STAGES = 4
PIECES = (1, 1, 2, 2, 1, 1)
SUMS = (2, 6)


def side_pairs(tiles, mems, step):
    pairs = []
    for mem in range(mems):
        for tile in range(tiles):
            source = tile + step
            if 0 <= source < tiles:
                crossed = (min(tile, source) % 2) == 1
                source_mem = mems - 1 - mem if crossed else mem
                pairs.append((source_mem * tiles + source, mem * tiles + tile))
    return pairs


def pick_body(source, picked, stage, sems, *, partner):
    size = picked.shape[1]
    mem = lax.axis_index("mem")
    start = pl.multiple_of((1 - mem if partner else mem) * size, size)
    rows = picked.shape[0] // STAGES
    inward, outward = [], []
    for k in range(STAGES):
        at = pl.ds(k * rows, rows)
        inward.append(
            pltpu.make_async_copy(
                source.at[at, pl.ds(start, size)], stage.at[at, :], sems.at[0, k]
            )
        )
        outward.append(pltpu.make_async_copy(stage.at[at, :], picked.at[at, :], sems.at[1, k]))
        inward[k].start()
    for k in range(STAGES):
        inward[k].wait()
        outward[k].start()
    for k in range(STAGES):
        outward[k].wait()


def pick_half(source, partner):
    rows, cols = source.shape
    return pl.pallas_call(
        functools.partial(pick_body, partner=partner),
        in_specs=[pl.BlockSpec(memory_space=pl.ANY)],
        out_specs=pl.BlockSpec(memory_space=pl.ANY),
        scratch_shapes=[
            pltpu.VMEM((rows, cols // 2), source.dtype),
            pltpu.SemaphoreType.DMA((2, STAGES)),
        ],
        out_shape=jax.ShapeDtypeStruct((rows, cols // 2), source.dtype),
        cost_estimate=pl.CostEstimate(
            flops=0, bytes_accessed=2 * source.size, transcendentals=0
        ),
        compiler_params=pltpu.CompilerParams(vmem_limit_bytes=4 << 20),
        name="pick_partner" if partner else "pick_own",
    )(pltpu.with_memory_space_constraint(source, pltpu.HBM))


def locate(lists, meta, row, n, blocks_dev):
    mem, tile = meta[0], meta[1]
    parity = lax.rem(tile, 2)
    local = lists[n, row] - (tile - 1) * blocks_dev
    which = lax.div(local, blocks_dev)
    inside = local - which * blocks_dev
    crossed = ((which == 0) & (parity == 0)) | ((which == 2) & (parity == 1))
    source = jnp.where(crossed, 1 - mem, mem)
    part = lax.div(inside, blocks_dev // 2)
    return which, inside, source, part == source, inside - part * (blocks_dev // 2)


def split(value):
    high = value.astype(jnp.bfloat16)
    return high, (value - high.astype(jnp.float32)).astype(jnp.bfloat16)


def dot(left, right):
    return lax.dot_general(
        left, right, (((1,), (0,)), ((), ())), preferred_element_type=jnp.float32
    )


def dot3(left, right):
    lh, ll = left
    rh, rl = right
    return dot(lh, rh) + (dot(lh, rl) + dot(ll, rh))


def parts3(value):
    high = value.astype(jnp.bfloat16)
    mid, low = split(value - high.astype(jnp.float32))
    return [high, mid, low]


def fetch(lists, meta, owner, block, tiles, raw, sems, blocks_dev, width):
    nloc, count = lists.shape
    rows = tiles[0].shape[0]
    for n in range(nloc):
        which, _, source, here, index = locate(
            lists, meta, owner * (count // 2) + block, n, blocks_dev
        )
        start = pl.multiple_of(index * width, width)
        at = pl.ds(n * width, width)
        first = pl.multiple_of(jnp.where(source == owner, 0, rows), rows)
        second = pl.multiple_of(jnp.where(source == owner, rows, 0), rows)
        for k in range(3):

            @pl.when(here & (which == k))
            def _(k=k, at=at, start=start, first=first, second=second):
                for part, place in ((tiles[2 * k], first), (tiles[2 * k + 1], second)):
                    pltpu.make_async_copy(
                        part.at[:, pl.ds(start, width)],
                        raw.at[block, pl.ds(place, rows), at],
                        sems.at[block],
                    ).start()


def local_gram(
    lists, meta, owner, block, raw, sems, low, own, high, ybuf, sbuf, blocks_dev, width
):
    nloc, count = lists.shape
    members = raw.shape[1]
    row = owner * (count // 2) + block
    found = [locate(lists, meta, row, n, blocks_dev) for n in range(nloc)]
    for n in range(nloc):

        @pl.when(found[n][3])
        def _():
            whole = raw.at[block, :, pl.ds(0, width)]
            pltpu.make_async_copy(whole, whole, sems.at[block]).wait()

    for n in range(nloc):
        which, inside, _, here, _ = found[n]
        at = pl.ds(n * width, width)

        @pl.when(jnp.logical_not(here))
        def _(at=at):
            ybuf[:, at] = jnp.zeros((members + ROWS, width), jnp.bfloat16)
            sbuf[:, at] = jnp.zeros((members, width), jnp.bfloat16)

        @pl.when(here)
        def _(at=at, which=which, inside=inside):
            values = raw[block, :, at].astype(jnp.float32)
            mean = jnp.sum(values, axis=0, keepdims=True) / members

            def entry(index):
                at_low = low[pl.ds(index, 1), :]
                at_own = own[pl.ds(index, 1), :]
                at_high = high[pl.ds(index, 1), :]
                return jnp.where(which == 0, at_low, jnp.where(which == 1, at_own, at_high))

            value = entry(inside)
            weight = entry(inside + blocks_dev)
            ybuf[pl.ds(members, ROWS), at] = jnp.concatenate(
                [*parts3(value - mean), jnp.zeros((ROWS - 3, width), jnp.bfloat16)], axis=0
            )
            pert = (values - mean).astype(jnp.bfloat16)
            ybuf[pl.ds(0, members), at] = pert
            sbuf[:, at] = (pert.astype(jnp.float32) * weight).astype(jnp.bfloat16)

    gram = lax.dot_general(
        ybuf[...], sbuf[...], (((1,), (1,)), ((), ())), preferred_element_type=jnp.float32
    )
    return gram[:members], jnp.sum(gram[members:], axis=0, keepdims=True)


def on_diagonal(size):
    return lax.broadcasted_iota(jnp.int32, (size, size), 0) == lax.broadcasted_iota(
        jnp.int32, (size, size), 1
    )


def sums_body(lists, meta, *refs, for_self, blocks_dev, width):
    tiles, (low, own, high) = refs[:6], refs[6:9]
    outs = refs[9:-4]
    raw, sems, ybuf, sbuf = refs[-4:]
    owner = meta[0] if for_self else 1 - meta[0]
    block = pl.program_id(0)
    blocks = raw.shape[0]

    @pl.when(block == 0)
    def _():
        for early in range(AHEAD):
            fetch(lists, meta, owner, early, tiles, raw, sems, blocks_dev, width)

    @pl.when(block + AHEAD < blocks)
    def _():
        fetch(lists, meta, owner, block + AHEAD, tiles, raw, sems, blocks_dev, width)

    matrix, rhs = local_gram(
        lists, meta, owner, block, raw, sems, low, own, high, ybuf, sbuf, blocks_dev, width
    )
    members = matrix.shape[0]
    if for_self:
        outs[0][0] = matrix
        outs[1][0] = jnp.broadcast_to(rhs, outs[1].shape[1:])
        return
    groups = members // ROWS
    diagonal = jnp.sum(jnp.where(on_diagonal(members), matrix, 0.0), axis=0, keepdims=True)
    lane = lax.broadcasted_iota(jnp.int32, (ROWS, members), 1)
    packed = [matrix[:ROWS]]
    for group in range(1, groups // 2):
        filled = pltpu.roll(matrix[members - group * ROWS :][:ROWS], group * ROWS, 1)
        packed.append(
            jnp.where(lane < group * ROWS, filled, matrix[group * ROWS : (group + 1) * ROWS])
        )
    middle = matrix[members // 2 : members // 2 + ROWS, members // 2 :]
    last = [jnp.concatenate([middle[ROWS // 2 :], middle[: ROWS // 2]], axis=1)]
    last += [part.astype(jnp.float32) for part in parts3(rhs) + parts3(diagonal)]
    last.append(jnp.zeros((ROWS // 2 - 6, members), jnp.float32))
    packed.append(jnp.concatenate(last, axis=0))
    first = 0
    for out, size in zip(outs, SUMS):

        @pl.when((block >= first) & (block < first + size))
        def _(out=out):
            for group, rows in enumerate(packed):
                out[0, pl.ds(group * ROWS, ROWS), :] = rows.astype(jnp.bfloat16)

        first += size


def partial_sums(lists, meta, tiles, tables, for_self, blocks_dev, width):
    nloc, count = lists.shape
    half = count // 2
    members = 2 * tiles[0].shape[0]
    span = nloc * width
    table_spec = pl.BlockSpec(tables[0].shape, lambda i, *_: (0, 0))
    if for_self:
        shapes = [(half, members, members), (half, 8, members)]
        kind = jnp.float32
        out_specs = [pl.BlockSpec((1, *shape[1:]), lambda i, *_: (i, 0, 0)) for shape in shapes]
    else:
        shapes = [(size, members // 2 + ROWS, members) for size in SUMS]
        kind = jnp.bfloat16
        out_specs = [
            pl.BlockSpec(
                (1, *shape[1:]),
                lambda i, *_, first=sum(SUMS[:k]), size=SUMS[k]: (
                    jnp.clip(i - first, 0, size - 1), 0, 0,
                ),
            )
            for k, shape in enumerate(shapes)
        ]
    return pl.pallas_call(
        functools.partial(sums_body, for_self=for_self, blocks_dev=blocks_dev, width=width),
        grid_spec=pltpu.PrefetchScalarGridSpec(
            num_scalar_prefetch=2,
            grid=(half,),
            in_specs=[pl.BlockSpec(memory_space=pl.ANY)] * 6 + [table_spec] * 3,
            out_specs=out_specs,
            scratch_shapes=[
                pltpu.VMEM((half, members, span), jnp.bfloat16),
                pltpu.SemaphoreType.DMA((half,)),
                pltpu.VMEM((members + ROWS, span), jnp.bfloat16),
                pltpu.VMEM((members, span), jnp.bfloat16),
            ],
        ),
        out_shape=[jax.ShapeDtypeStruct(shape, kind) for shape in shapes],
        cost_estimate=pl.CostEstimate(
            flops=2 * half * members * members * span,
            bytes_accessed=2 * members * half * span,
            transcendentals=0,
        ),
        compiler_params=pltpu.CompilerParams(vmem_limit_bytes=20 << 20),
        name="sums_self" if for_self else "sums_send",
    )(lists, meta, *tiles, *tables)


def analysis_body(meta, mine, theirs, ours, our_rhs, received, *refs, width):
    kept, sent, ubuf, xbuf, mbuf = refs[-5:]
    rows = mine.shape[1]
    members = 2 * rows

    matrix = ours[0]
    rhs = our_rhs[0, pl.ds(0, 1), :]
    groups = members // ROWS
    ubuf[pl.ds(0, ROWS), :] = received[0, pl.ds(0, ROWS), :].astype(jnp.float32)
    for group in range(1, groups // 2):
        piece = received[0, pl.ds(group * ROWS, ROWS), :].astype(jnp.float32)
        ubuf[pl.ds(group * ROWS, ROWS), :] = piece
        ubuf[pl.ds(members - group * ROWS, ROWS), :] = pltpu.roll(
            piece, members - group * ROWS, 1
        )
    last = received[0, pl.ds(members // 2, ROWS), :].astype(jnp.float32)
    step = ROWS // 2
    ubuf[pl.ds(members // 2, step), pl.ds(rows, rows)] = last[:step, rows:]
    ubuf[pl.ds(members // 2 + step, step), pl.ds(rows, rows)] = last[:step, :rows]
    rhs = rhs + jnp.sum(last[step : step + 3], axis=0, keepdims=True)
    upper = ubuf[...]
    block_row = lax.div(lax.broadcasted_iota(jnp.int32, (members, members), 0), ROWS)
    block_col = lax.div(lax.broadcasted_iota(jnp.int32, (members, members), 1), ROWS)
    other = jnp.where(block_row <= block_col, upper, upper.T)
    diagonal = on_diagonal(members)
    other = jnp.where(diagonal, jnp.sum(last[step + 3 : step + 6], axis=0, keepdims=True), other)
    matrix = matrix + other
    matrix = matrix + jnp.where(diagonal, members - 1.0, 0.0)
    trace = jnp.sum(
        jnp.sum(jnp.where(diagonal, matrix, 0.0), axis=0, keepdims=True), axis=1, keepdims=True
    )
    scale = trace / members
    iterate = matrix / scale
    eye15 = jnp.where(diagonal, 1.5, 0.0)
    inverse_root = eye15 - 0.5 * iterate
    factor = split(inverse_root)
    iterate = dot3(factor, split(iterate))
    for step in range(1, NSTEPS):
        root_parts = split(inverse_root)
        iterate_parts = split(iterate)
        factor = split(eye15 - 0.5 * dot3(iterate_parts, root_parts))
        if step + 1 < NSTEPS:
            iterate = dot3(factor, iterate_parts)
        inverse_root = dot3(root_parts, factor)
    root_parts = split(inverse_root)
    shift = jnp.broadcast_to(rhs, (ROWS, members))
    shift = dot3(split(shift), root_parts)
    shift = dot3(split(shift), root_parts)[:1] / scale
    trans = (jnp.sqrt((members - 1.0) / scale) * inverse_root + shift).astype(jnp.bfloat16)

    layers = mine.shape[0]
    for layer in range(layers):
        at = pl.ds(layer * width, width)
        first = mine[layer].astype(jnp.float32)
        second = theirs[layer].astype(jnp.float32)
        mean = (
            jnp.sum(first, axis=0, keepdims=True) + jnp.sum(second, axis=0, keepdims=True)
        ) / members
        mbuf[:, at] = mean
        xbuf[pl.ds(0, rows), at] = (first - mean).astype(jnp.bfloat16)
        xbuf[pl.ds(rows, rows), at] = (second - mean).astype(jnp.bfloat16)
    result = (dot(trans, xbuf[...]) + mbuf[...]).astype(jnp.bfloat16)
    for layer in range(layers):
        at = slice(layer * width, (layer + 1) * width)
        kept[layer] = result[:rows, at]
        sent[layer] = result[rows:, at]


def analyse(meta, mine, theirs, ours, our_rhs, received, output, first, size, skipped, width):
    layers, rows, cols = mine.shape
    members = 2 * rows
    half = cols // 2 // width
    flops = 2 * size * members * members * (18 * members + layers * width)

    def mine_at(i, meta):
        return (0, 0, meta[0] * half + first + i)

    tile_block = (layers, rows, width)
    in_specs = [
        pl.BlockSpec(tile_block, mine_at),
        pl.BlockSpec(tile_block, lambda i, *_: (0, 0, first + i)),
        pl.BlockSpec((1, *ours.shape[1:]), lambda i, *_: (first + i, 0, 0)),
        pl.BlockSpec((1, *our_rhs.shape[1:]), lambda i, *_: (first + i, 0, 0)),
        pl.BlockSpec((1, *received.shape[1:]), lambda i, *_: (first - skipped + i, 0, 0)),
    ]
    operands = [mine, theirs, ours, our_rhs, received]
    aliases = {}
    if output is not None:
        in_specs.append(pl.BlockSpec(memory_space=pl.ANY))
        aliases = {1 + len(operands): 0}
        operands.append(output)
    return pl.pallas_call(
        functools.partial(analysis_body, width=width),
        grid_spec=pltpu.PrefetchScalarGridSpec(
            num_scalar_prefetch=1,
            grid=(size,),
            in_specs=in_specs,
            out_specs=[
                pl.BlockSpec(tile_block, mine_at),
                pl.BlockSpec(tile_block, lambda i, *_: (0, 0, i)),
            ],
            scratch_shapes=[
                pltpu.VMEM((members, members), jnp.float32),
                pltpu.VMEM((members, layers * width), jnp.bfloat16),
                pltpu.VMEM((1, layers * width), jnp.float32),
            ],
        ),
        out_shape=[
            jax.ShapeDtypeStruct(mine.shape, jnp.bfloat16),
            jax.ShapeDtypeStruct((layers, rows, size * width), jnp.bfloat16),
        ],
        input_output_aliases=aliases,
        cost_estimate=pl.CostEstimate(
            flops=flops, bytes_accessed=size * 8 * rows * layers * width, transcendentals=0
        ),
        compiler_params=pltpu.CompilerParams(vmem_limit_bytes=20 << 20),
        name="analyse",
    )(meta, *operands)


def place_body(meta, piece, output, placed, sem, *, first, width):
    start = pl.multiple_of((1 - meta[0]) * (placed.shape[2] // 2) + first * width, width)
    copy = pltpu.make_async_copy(piece, placed.at[:, :, pl.ds(start, piece.shape[2])], sem)
    copy.start()
    copy.wait()


def place(meta, piece, output, first, width):
    return pl.pallas_call(
        functools.partial(place_body, first=first, width=width),
        grid_spec=pltpu.PrefetchScalarGridSpec(
            num_scalar_prefetch=1,
            grid=(1,),
            in_specs=[pl.BlockSpec(memory_space=pl.ANY)] * 2,
            out_specs=pl.BlockSpec(memory_space=pl.ANY),
            scratch_shapes=[pltpu.SemaphoreType.DMA],
        ),
        out_shape=jax.ShapeDtypeStruct(output.shape, output.dtype),
        input_output_aliases={2: 0},
        cost_estimate=pl.CostEstimate(
            flops=0, bytes_accessed=4 * piece.size, transcendentals=0
        ),
        compiler_params=pltpu.CompilerParams(vmem_limit_bytes=2 << 20),
        name="place",
    )(meta, piece, output)


def per_device(
    prior_members,
    members_in_reading_space,
    measured_values,
    obs_precision_weights,
    valid_reading_numbers,
    neighbour_lists,
):
    tile_no = lax.axis_index("tile")
    member_no = lax.axis_index("mem")
    tiles = lax.axis_size("tile")
    mems = lax.axis_size("mem")
    both = ("mem", "tile")
    swap = [(0, 1), (1, 0)]
    from_low = side_pairs(tiles, mems, -1)
    from_high = side_pairs(tiles, mems, 1)
    blocks_dev = valid_reading_numbers.shape[0]
    width = members_in_reading_space.shape[1] // blocks_dev
    cols = prior_members.shape[2]

    mine = jnp.transpose(prior_members, (1, 0, 2))
    lists = neighbour_lists.T
    meta = jnp.stack([member_no, tile_no]).astype(jnp.int32)

    obs = members_in_reading_space
    swapped = lax.ppermute(pick_half(obs, True), "mem", swap)
    own_set = pick_half(obs, False)
    low_own = lax.ppermute(own_set, both, from_low)
    high_own = lax.ppermute(own_set, both, from_high)
    half = cols // 2
    outgoing = lax.dynamic_slice_in_dim(mine, (1 - member_no) * half, half, 2)
    theirs = lax.ppermute(outgoing, "mem", swap)
    low_other = lax.ppermute(swapped, both, from_low)
    high_other = lax.ppermute(swapped, both, from_high)
    tiles_held = (low_own, low_other, own_set, swapped, high_own, high_other)
    slots = jnp.arange(width, dtype=jnp.int32)
    valid = slots[None, :] < valid_reading_numbers[:, None]
    weight = jnp.where(valid, obs_precision_weights.reshape(blocks_dev, width), 0.0)
    table = jnp.concatenate([measured_values.reshape(blocks_dev, width), weight], axis=0)
    table_low = lax.ppermute(table, both, from_low)
    table_high = lax.ppermute(table, both, from_high)
    tables = (table_low, table, table_high)

    sums = partial_sums(lists, meta, tiles_held, tables, False, blocks_dev, width)
    received = []
    for piece in sums:
        received.append(lax.ppermute(piece, "mem", swap))
    ours, our_rhs = partial_sums(lists, meta, tiles_held, tables, True, blocks_dev, width)
    output = None
    arrived = []
    for k, size in enumerate(PIECES):
        first = sum(PIECES[:k])
        late = first >= SUMS[0]
        output, sent = analyse(
            meta, mine, theirs, ours, our_rhs, received[late], output, first, size,
            SUMS[0] if late else 0, width,
        )
        arrived.append(lax.ppermute(sent, "mem", swap))
    for k, piece in enumerate(arrived):
        output = place(meta, piece, output, sum(PIECES[:k]), width)
    return jnp.transpose(output, (1, 0, 2))


def solution(mesh):
    in_specs = (
        P("mem", None, "tile"),
        P("mem", "tile"),
        P("tile"),
        P("tile"),
        P("tile"),
        P("tile", None),
    )
    out_specs = P("mem", None, "tile")

    return jax.shard_map(
        per_device, mesh=mesh, in_specs=in_specs, out_specs=out_specs, check_vma=False
    )
```

```python
import functools

import jax
import jax.numpy as jnp
from jax import lax
from jax.experimental import pallas as pl
from jax.experimental.pallas import tpu as pltpu
from jax.sharding import PartitionSpec as P


NSTEPS = 3
ROWS = 16
AHEAD = 3
PIECES = (1, 1, 2, 2, 1, 1)
SUMS = (2, 6)


def side_pairs(tiles, mems, step):
    pairs = []
    for mem in range(mems):
        for tile in range(tiles):
            source = tile + step
            if 0 <= source < tiles:
                crossed = (min(tile, source) % 2) == 1
                source_mem = mems - 1 - mem if crossed else mem
                pairs.append((source_mem * tiles + source, mem * tiles + tile))
    return pairs


def pick_body(source, *refs, partner):
    picked, sem = refs[-2:]
    size = picked.shape[1]
    mem = lax.axis_index("mem")
    start = pl.multiple_of((1 - mem if partner else mem) * size, size)
    copy = pltpu.make_async_copy(source.at[:, pl.ds(start, size)], picked, sem)
    copy.start()
    copy.wait()


def pick_half(source, partner, *after):
    rows, cols = source.shape
    return pl.pallas_call(
        functools.partial(pick_body, partner=partner),
        in_specs=[pl.BlockSpec(memory_space=pl.ANY)] * (1 + len(after)),
        out_specs=pl.BlockSpec(memory_space=pl.ANY),
        scratch_shapes=[pltpu.SemaphoreType.DMA],
        out_shape=jax.ShapeDtypeStruct((rows, cols // 2), source.dtype),
        cost_estimate=pl.CostEstimate(
            flops=0, bytes_accessed=2 * source.size, transcendentals=0
        ),
        compiler_params=pltpu.CompilerParams(vmem_limit_bytes=4 << 20),
        name="pick_partner" if partner else "pick_own",
    )(pltpu.with_memory_space_constraint(source, pltpu.HBM), *after)


def locate(lists, meta, row, n, blocks_dev):
    mem, tile = meta[0], meta[1]
    parity = lax.rem(tile, 2)
    local = lists[n, row] - (tile - 1) * blocks_dev
    which = lax.div(local, blocks_dev)
    inside = local - which * blocks_dev
    crossed = ((which == 0) & (parity == 0)) | ((which == 2) & (parity == 1))
    source = jnp.where(crossed, 1 - mem, mem)
    part = lax.div(inside, blocks_dev // 2)
    return which, inside, source, part == source, inside - part * (blocks_dev // 2)


def split(value):
    high = value.astype(jnp.bfloat16)
    return high, (value - high.astype(jnp.float32)).astype(jnp.bfloat16)


def dot(left, right):
    return lax.dot_general(
        left, right, (((1,), (0,)), ((), ())), preferred_element_type=jnp.float32
    )


def dot3(left, right):
    lh, ll = left
    rh, rl = right
    return dot(lh, rh) + (dot(lh, rl) + dot(ll, rh))


def parts3(value):
    high = value.astype(jnp.bfloat16)
    mid, low = split(value - high.astype(jnp.float32))
    return [high, mid, low]


def fetch(lists, meta, owner, block, tiles, raw, sems, blocks_dev, width):
    nloc, count = lists.shape
    rows = tiles[0].shape[0]
    for n in range(nloc):
        which, _, source, here, index = locate(
            lists, meta, owner * (count // 2) + block, n, blocks_dev
        )
        start = pl.multiple_of(index * width, width)
        at = pl.ds(n * width, width)
        first = pl.multiple_of(jnp.where(source == owner, 0, rows), rows)
        second = pl.multiple_of(jnp.where(source == owner, rows, 0), rows)
        for k in range(3):

            @pl.when(here & (which == k))
            def _(k=k, at=at, start=start, first=first, second=second):
                for part, place in ((tiles[2 * k], first), (tiles[2 * k + 1], second)):
                    pltpu.make_async_copy(
                        part.at[:, pl.ds(start, width)],
                        raw.at[block, pl.ds(place, rows), at],
                        sems.at[block],
                    ).start()


def local_gram(
    lists, meta, owner, block, raw, sems, low, own, high, ybuf, sbuf, blocks_dev, width
):
    nloc, count = lists.shape
    members = raw.shape[1]
    row = owner * (count // 2) + block
    found = [locate(lists, meta, row, n, blocks_dev) for n in range(nloc)]
    for n in range(nloc):

        @pl.when(found[n][3])
        def _():
            whole = raw.at[block, :, pl.ds(0, width)]
            pltpu.make_async_copy(whole, whole, sems.at[block]).wait()

    for n in range(nloc):
        which, inside, _, here, _ = found[n]
        at = pl.ds(n * width, width)

        @pl.when(jnp.logical_not(here))
        def _(at=at):
            ybuf[:, at] = jnp.zeros((members + ROWS, width), jnp.bfloat16)
            sbuf[:, at] = jnp.zeros((members, width), jnp.bfloat16)

        @pl.when(here)
        def _(at=at, which=which, inside=inside):
            values = raw[block, :, at].astype(jnp.float32)
            mean = jnp.sum(values, axis=0, keepdims=True) / members

            def entry(index):
                at_low = low[pl.ds(index, 1), :]
                at_own = own[pl.ds(index, 1), :]
                at_high = high[pl.ds(index, 1), :]
                return jnp.where(which == 0, at_low, jnp.where(which == 1, at_own, at_high))

            value = entry(inside)
            weight = entry(inside + blocks_dev)
            ybuf[pl.ds(members, ROWS), at] = jnp.concatenate(
                [*parts3(value - mean), jnp.zeros((ROWS - 3, width), jnp.bfloat16)], axis=0
            )
            pert = (values - mean).astype(jnp.bfloat16)
            ybuf[pl.ds(0, members), at] = pert
            sbuf[:, at] = (pert.astype(jnp.float32) * weight).astype(jnp.bfloat16)

    gram = lax.dot_general(
        ybuf[...], sbuf[...], (((1,), (1,)), ((), ())), preferred_element_type=jnp.float32
    )
    return gram[:members], jnp.sum(gram[members:], axis=0, keepdims=True)


def on_diagonal(size):
    return lax.broadcasted_iota(jnp.int32, (size, size), 0) == lax.broadcasted_iota(
        jnp.int32, (size, size), 1
    )


def sums_body(lists, meta, *refs, for_self, blocks_dev, width):
    tiles, (low, own, high) = refs[:6], refs[6:9]
    outs = refs[9:-4]
    raw, sems, ybuf, sbuf = refs[-4:]
    owner = meta[0] if for_self else 1 - meta[0]
    block = pl.program_id(0)
    blocks = raw.shape[0]

    @pl.when(block == 0)
    def _():
        for early in range(AHEAD):
            fetch(lists, meta, owner, early, tiles, raw, sems, blocks_dev, width)

    @pl.when(block + AHEAD < blocks)
    def _():
        fetch(lists, meta, owner, block + AHEAD, tiles, raw, sems, blocks_dev, width)

    matrix, rhs = local_gram(
        lists, meta, owner, block, raw, sems, low, own, high, ybuf, sbuf, blocks_dev, width
    )
    members = matrix.shape[0]
    if for_self:
        outs[0][0] = matrix
        outs[1][0] = jnp.broadcast_to(rhs, outs[1].shape[1:])
        return
    groups = members // ROWS
    diagonal = jnp.sum(jnp.where(on_diagonal(members), matrix, 0.0), axis=0, keepdims=True)
    matrix = 0.5 * (matrix + matrix.T)
    lane = lax.broadcasted_iota(jnp.int32, (ROWS, members), 1)
    packed = [matrix[:ROWS]]
    for group in range(1, groups // 2):
        filled = pltpu.roll(matrix[members - group * ROWS :][:ROWS], group * ROWS, 1)
        packed.append(
            jnp.where(lane < group * ROWS, filled, matrix[group * ROWS : (group + 1) * ROWS])
        )
    middle = matrix[members // 2 : members // 2 + ROWS, members // 2 :]
    last = [jnp.concatenate([middle[ROWS // 2 :], middle[: ROWS // 2]], axis=1)]
    last += [part.astype(jnp.float32) for part in parts3(rhs) + parts3(diagonal)]
    last.append(jnp.zeros((ROWS // 2 - 6, members), jnp.float32))
    packed.append(jnp.concatenate(last, axis=0))
    first = 0
    for out, size in zip(outs, SUMS):

        @pl.when((block >= first) & (block < first + size))
        def _(out=out):
            for group, rows in enumerate(packed):
                out[0, pl.ds(group * ROWS, ROWS), :] = rows.astype(jnp.bfloat16)

        first += size


def partial_sums(lists, meta, tiles, tables, for_self, blocks_dev, width):
    nloc, count = lists.shape
    half = count // 2
    members = 2 * tiles[0].shape[0]
    span = nloc * width
    table_spec = pl.BlockSpec(tables[0].shape, lambda i, *_: (0, 0))
    if for_self:
        shapes = [(half, members, members), (half, 8, members)]
        kind = jnp.float32
        out_specs = [pl.BlockSpec((1, *shape[1:]), lambda i, *_: (i, 0, 0)) for shape in shapes]
    else:
        shapes = [(size, members // 2 + ROWS, members) for size in SUMS]
        kind = jnp.bfloat16
        out_specs = [
            pl.BlockSpec(
                (1, *shape[1:]),
                lambda i, *_, first=sum(SUMS[:k]), size=SUMS[k]: (
                    jnp.clip(i - first, 0, size - 1), 0, 0,
                ),
            )
            for k, shape in enumerate(shapes)
        ]
    return pl.pallas_call(
        functools.partial(sums_body, for_self=for_self, blocks_dev=blocks_dev, width=width),
        grid_spec=pltpu.PrefetchScalarGridSpec(
            num_scalar_prefetch=2,
            grid=(half,),
            in_specs=[pl.BlockSpec(memory_space=pl.ANY)] * 6 + [table_spec] * 3,
            out_specs=out_specs,
            scratch_shapes=[
                pltpu.VMEM((half, members, span), jnp.bfloat16),
                pltpu.SemaphoreType.DMA((half,)),
                pltpu.VMEM((members + ROWS, span), jnp.bfloat16),
                pltpu.VMEM((members, span), jnp.bfloat16),
            ],
        ),
        out_shape=[jax.ShapeDtypeStruct(shape, kind) for shape in shapes],
        cost_estimate=pl.CostEstimate(
            flops=2 * half * members * members * span,
            bytes_accessed=2 * members * half * span,
            transcendentals=0,
        ),
        compiler_params=pltpu.CompilerParams(vmem_limit_bytes=20 << 20),
        name="sums_self" if for_self else "sums_send",
    )(lists, meta, *tiles, *tables)


def analysis_body(meta, mine, theirs, ours, our_rhs, received, *refs, width):
    kept, sent, ubuf, xbuf, mbuf = refs[-5:]
    rows = mine.shape[1]
    members = 2 * rows

    matrix = ours[0]
    rhs = our_rhs[0, pl.ds(0, 1), :]
    groups = members // ROWS
    ubuf[pl.ds(0, ROWS), :] = received[0, pl.ds(0, ROWS), :].astype(jnp.float32)
    for group in range(1, groups // 2):
        piece = received[0, pl.ds(group * ROWS, ROWS), :].astype(jnp.float32)
        ubuf[pl.ds(group * ROWS, ROWS), :] = piece
        ubuf[pl.ds(members - group * ROWS, ROWS), :] = pltpu.roll(
            piece, members - group * ROWS, 1
        )
    last = received[0, pl.ds(members // 2, ROWS), :].astype(jnp.float32)
    step = ROWS // 2
    ubuf[pl.ds(members // 2, step), pl.ds(rows, rows)] = last[:step, rows:]
    ubuf[pl.ds(members // 2 + step, step), pl.ds(rows, rows)] = last[:step, :rows]
    rhs = rhs + jnp.sum(last[step : step + 3], axis=0, keepdims=True)
    upper = ubuf[...]
    block_row = lax.div(lax.broadcasted_iota(jnp.int32, (members, members), 0), ROWS)
    block_col = lax.div(lax.broadcasted_iota(jnp.int32, (members, members), 1), ROWS)
    other = jnp.where(block_row <= block_col, upper, upper.T)
    diagonal = on_diagonal(members)
    other = jnp.where(diagonal, jnp.sum(last[step + 3 : step + 6], axis=0, keepdims=True), other)
    matrix = matrix + other
    matrix = matrix + jnp.where(diagonal, members - 1.0, 0.0)
    trace = jnp.sum(
        jnp.sum(jnp.where(diagonal, matrix, 0.0), axis=0, keepdims=True), axis=1, keepdims=True
    )
    scale = trace / members
    iterate = matrix / scale
    eye15 = jnp.where(diagonal, 1.5, 0.0)
    inverse_root = eye15 - 0.5 * iterate
    factor = split(inverse_root)
    iterate = dot3(factor, split(iterate))
    for step in range(1, NSTEPS):
        root_parts = split(inverse_root)
        iterate_parts = split(iterate)
        factor = split(eye15 - 0.5 * dot3(iterate_parts, root_parts))
        if step + 1 < NSTEPS:
            iterate = dot3(factor, iterate_parts)
        inverse_root = dot3(root_parts, factor)
    root_parts = split(inverse_root)
    shift = jnp.broadcast_to(rhs, (ROWS, members))
    shift = dot3(split(shift), root_parts)
    shift = dot3(split(shift), root_parts)[:1] / scale
    trans = (jnp.sqrt((members - 1.0) / scale) * inverse_root + shift).astype(jnp.bfloat16)

    layers = mine.shape[0]
    for layer in range(layers):
        at = pl.ds(layer * width, width)
        first = mine[layer].astype(jnp.float32)
        second = theirs[layer].astype(jnp.float32)
        mean = (
            jnp.sum(first, axis=0, keepdims=True) + jnp.sum(second, axis=0, keepdims=True)
        ) / members
        mbuf[:, at] = mean
        xbuf[pl.ds(0, rows), at] = (first - mean).astype(jnp.bfloat16)
        xbuf[pl.ds(rows, rows), at] = (second - mean).astype(jnp.bfloat16)
    result = (dot(trans, xbuf[...]) + mbuf[...]).astype(jnp.bfloat16)
    for layer in range(layers):
        at = slice(layer * width, (layer + 1) * width)
        kept[layer] = result[:rows, at]
        sent[layer] = result[rows:, at]


def analyse(meta, mine, theirs, ours, our_rhs, received, output, first, size, skipped, width):
    layers, rows, cols = mine.shape
    members = 2 * rows
    half = cols // 2 // width
    flops = 2 * size * members * members * (18 * members + layers * width)

    def mine_at(i, meta):
        return (0, 0, meta[0] * half + first + i)

    tile_block = (layers, rows, width)
    in_specs = [
        pl.BlockSpec(tile_block, mine_at),
        pl.BlockSpec(tile_block, lambda i, *_: (0, 0, first + i)),
        pl.BlockSpec((1, *ours.shape[1:]), lambda i, *_: (first + i, 0, 0)),
        pl.BlockSpec((1, *our_rhs.shape[1:]), lambda i, *_: (first + i, 0, 0)),
        pl.BlockSpec((1, *received.shape[1:]), lambda i, *_: (first - skipped + i, 0, 0)),
    ]
    operands = [mine, theirs, ours, our_rhs, received]
    aliases = {}
    if output is not None:
        in_specs.append(pl.BlockSpec(memory_space=pl.ANY))
        aliases = {1 + len(operands): 0}
        operands.append(output)
    return pl.pallas_call(
        functools.partial(analysis_body, width=width),
        grid_spec=pltpu.PrefetchScalarGridSpec(
            num_scalar_prefetch=1,
            grid=(size,),
            in_specs=in_specs,
            out_specs=[
                pl.BlockSpec(tile_block, mine_at),
                pl.BlockSpec(tile_block, lambda i, *_: (0, 0, i)),
            ],
            scratch_shapes=[
                pltpu.VMEM((members, members), jnp.float32),
                pltpu.VMEM((members, layers * width), jnp.bfloat16),
                pltpu.VMEM((1, layers * width), jnp.float32),
            ],
        ),
        out_shape=[
            jax.ShapeDtypeStruct(mine.shape, jnp.bfloat16),
            jax.ShapeDtypeStruct((layers, rows, size * width), jnp.bfloat16),
        ],
        input_output_aliases=aliases,
        cost_estimate=pl.CostEstimate(
            flops=flops, bytes_accessed=size * 8 * rows * layers * width, transcendentals=0
        ),
        compiler_params=pltpu.CompilerParams(vmem_limit_bytes=20 << 20),
        name="analyse",
    )(meta, *operands)


def place_body(meta, piece, output, placed, sem, *, first, width):
    start = pl.multiple_of((1 - meta[0]) * (placed.shape[2] // 2) + first * width, width)
    copy = pltpu.make_async_copy(piece, placed.at[:, :, pl.ds(start, piece.shape[2])], sem)
    copy.start()
    copy.wait()


def place(meta, piece, output, first, width):
    return pl.pallas_call(
        functools.partial(place_body, first=first, width=width),
        grid_spec=pltpu.PrefetchScalarGridSpec(
            num_scalar_prefetch=1,
            grid=(1,),
            in_specs=[pl.BlockSpec(memory_space=pl.ANY)] * 2,
            out_specs=pl.BlockSpec(memory_space=pl.ANY),
            scratch_shapes=[pltpu.SemaphoreType.DMA],
        ),
        out_shape=jax.ShapeDtypeStruct(output.shape, output.dtype),
        input_output_aliases={2: 0},
        cost_estimate=pl.CostEstimate(
            flops=0, bytes_accessed=4 * piece.size, transcendentals=0
        ),
        compiler_params=pltpu.CompilerParams(vmem_limit_bytes=2 << 20),
        name="place",
    )(meta, piece, output)


def per_device(
    prior_members,
    members_in_reading_space,
    measured_values,
    obs_precision_weights,
    valid_reading_numbers,
    neighbour_lists,
):
    tile_no = lax.axis_index("tile")
    member_no = lax.axis_index("mem")
    tiles = lax.axis_size("tile")
    mems = lax.axis_size("mem")
    both = ("mem", "tile")
    swap = [(0, 1), (1, 0)]
    from_low = side_pairs(tiles, mems, -1)
    from_high = side_pairs(tiles, mems, 1)
    blocks_dev = valid_reading_numbers.shape[0]
    width = members_in_reading_space.shape[1] // blocks_dev
    cols = prior_members.shape[2]

    mine = jnp.transpose(prior_members, (1, 0, 2))
    lists = neighbour_lists.T
    meta = jnp.stack([member_no, tile_no]).astype(jnp.int32)

    obs = members_in_reading_space
    other_set = pick_half(obs, True)
    swapped = lax.ppermute(other_set, "mem", swap)
    own_set = pick_half(obs, False, other_set)
    low_own = lax.ppermute(own_set, both, from_low)
    high_own = lax.ppermute(own_set, both, from_high)
    half = cols // 2
    outgoing = lax.dynamic_slice_in_dim(mine, (1 - member_no) * half, half, 2)
    theirs = lax.ppermute(outgoing, "mem", swap)
    low_other = lax.ppermute(swapped, both, from_low)
    high_other = lax.ppermute(swapped, both, from_high)
    tiles_held = (low_own, low_other, own_set, swapped, high_own, high_other)
    slots = jnp.arange(width, dtype=jnp.int32)
    valid = slots[None, :] < valid_reading_numbers[:, None]
    weight = jnp.where(valid, obs_precision_weights.reshape(blocks_dev, width), 0.0)
    table = jnp.concatenate([measured_values.reshape(blocks_dev, width), weight], axis=0)
    table_low = lax.ppermute(table, both, from_low)
    table_high = lax.ppermute(table, both, from_high)
    tables = (table_low, table, table_high)

    sums = partial_sums(lists, meta, tiles_held, tables, False, blocks_dev, width)
    received = []
    for piece in sums:
        received.append(lax.ppermute(piece, "mem", swap))
    ours, our_rhs = partial_sums(lists, meta, tiles_held, tables, True, blocks_dev, width)
    output = None
    arrived = []
    for k, size in enumerate(PIECES):
        first = sum(PIECES[:k])
        late = first >= SUMS[0]
        output, sent = analyse(
            meta, mine, theirs, ours, our_rhs, received[late], output, first, size,
            SUMS[0] if late else 0, width,
        )
        arrived.append(lax.ppermute(sent, "mem", swap))
    for k, piece in enumerate(arrived):
        output = place(meta, piece, output, sum(PIECES[:k]), width)
    return jnp.transpose(output, (1, 0, 2))


def solution(mesh):
    in_specs = (
        P("mem", None, "tile"),
        P("mem", "tile"),
        P("tile"),
        P("tile"),
        P("tile"),
        P("tile", None),
    )
    out_specs = P("mem", None, "tile")

    return jax.shard_map(
        per_device, mesh=mesh, in_specs=in_specs, out_specs=out_specs, check_vma=False
    )
```

```python
import functools

import jax
import jax.numpy as jnp
from jax import lax
from jax.experimental import pallas as pl
from jax.experimental.pallas import tpu as pltpu
from jax.sharding import PartitionSpec as P


NSTEPS = 3
ROWS = 16
AHEAD = 3
PIECES = (1, 1, 2, 2, 1, 1)
SUMS = (2, 6)


def side_pairs(tiles, mems, step):
    pairs = []
    for mem in range(mems):
        for tile in range(tiles):
            source = tile + step
            if 0 <= source < tiles:
                crossed = (min(tile, source) % 2) == 1
                source_mem = mems - 1 - mem if crossed else mem
                pairs.append((source_mem * tiles + source, mem * tiles + tile))
    return pairs


def pick_body(source, *refs, partner):
    picked, sem = refs[-2:]
    size = picked.shape[1]
    mem = lax.axis_index("mem")
    start = pl.multiple_of((1 - mem if partner else mem) * size, size)
    copy = pltpu.make_async_copy(source.at[:, pl.ds(start, size)], picked, sem)
    copy.start()
    copy.wait()


def pick_half(source, partner, *after):
    rows, cols = source.shape
    return pl.pallas_call(
        functools.partial(pick_body, partner=partner),
        in_specs=[pl.BlockSpec(memory_space=pl.ANY)] * (1 + len(after)),
        out_specs=pl.BlockSpec(memory_space=pl.ANY),
        scratch_shapes=[pltpu.SemaphoreType.DMA],
        out_shape=jax.ShapeDtypeStruct((rows, cols // 2), source.dtype),
        cost_estimate=pl.CostEstimate(
            flops=0, bytes_accessed=2 * source.size, transcendentals=0
        ),
        compiler_params=pltpu.CompilerParams(vmem_limit_bytes=4 << 20),
        name="pick_partner" if partner else "pick_own",
    )(pltpu.with_memory_space_constraint(source, pltpu.HBM), *after)


def locate(lists, meta, row, n, blocks_dev):
    mem, tile = meta[0], meta[1]
    parity = lax.rem(tile, 2)
    local = lists[n, row] - (tile - 1) * blocks_dev
    which = lax.div(local, blocks_dev)
    inside = local - which * blocks_dev
    crossed = ((which == 0) & (parity == 0)) | ((which == 2) & (parity == 1))
    source = jnp.where(crossed, 1 - mem, mem)
    part = lax.div(inside, blocks_dev // 2)
    return which, inside, source, part == source, inside - part * (blocks_dev // 2)


def split(value):
    high = value.astype(jnp.bfloat16)
    return high, (value - high.astype(jnp.float32)).astype(jnp.bfloat16)


def dot(left, right):
    return lax.dot_general(
        left, right, (((1,), (0,)), ((), ())), preferred_element_type=jnp.float32
    )


def dot3(left, right):
    lh, ll = left
    rh, rl = right
    return dot(lh, rh) + (dot(lh, rl) + dot(ll, rh))


def parts3(value):
    high = value.astype(jnp.bfloat16)
    mid, low = split(value - high.astype(jnp.float32))
    return [high, mid, low]


def fetch(lists, meta, owner, block, tiles, raw, sems, blocks_dev, width):
    nloc, count = lists.shape
    rows = tiles[0].shape[0]
    for n in range(nloc):
        which, _, source, here, index = locate(
            lists, meta, owner * (count // 2) + block, n, blocks_dev
        )
        start = pl.multiple_of(index * width, width)
        at = pl.ds(n * width, width)
        first = pl.multiple_of(jnp.where(source == owner, 0, rows), rows)
        second = pl.multiple_of(jnp.where(source == owner, rows, 0), rows)
        for k in range(3):

            @pl.when(here & (which == k))
            def _(k=k, at=at, start=start, first=first, second=second):
                for part, place in ((tiles[2 * k], first), (tiles[2 * k + 1], second)):
                    pltpu.make_async_copy(
                        part.at[:, pl.ds(start, width)],
                        raw.at[block, pl.ds(place, rows), at],
                        sems.at[block],
                    ).start()


def local_gram(
    lists, meta, owner, block, raw, sems, low, own, high, ybuf, sbuf, blocks_dev, width
):
    nloc, count = lists.shape
    members = raw.shape[1]
    row = owner * (count // 2) + block
    found = [locate(lists, meta, row, n, blocks_dev) for n in range(nloc)]
    for n in range(nloc):

        @pl.when(found[n][3])
        def _():
            whole = raw.at[block, :, pl.ds(0, width)]
            pltpu.make_async_copy(whole, whole, sems.at[block]).wait()

    for n in range(nloc):
        which, inside, _, here, _ = found[n]
        at = pl.ds(n * width, width)

        @pl.when(jnp.logical_not(here))
        def _(at=at):
            ybuf[:, at] = jnp.zeros((members + ROWS, width), jnp.bfloat16)
            sbuf[:, at] = jnp.zeros((members, width), jnp.bfloat16)

        @pl.when(here)
        def _(at=at, which=which, inside=inside):
            values = raw[block, :, at].astype(jnp.float32)
            mean = jnp.sum(values, axis=0, keepdims=True) / members

            def entry(index):
                at_low = low[pl.ds(index, 1), :]
                at_own = own[pl.ds(index, 1), :]
                at_high = high[pl.ds(index, 1), :]
                return jnp.where(which == 0, at_low, jnp.where(which == 1, at_own, at_high))

            value = entry(inside)
            weight = entry(inside + blocks_dev)
            ybuf[pl.ds(members, ROWS), at] = jnp.concatenate(
                [*parts3(value - mean), jnp.zeros((ROWS - 3, width), jnp.bfloat16)], axis=0
            )
            pert = (values - mean).astype(jnp.bfloat16)
            ybuf[pl.ds(0, members), at] = pert
            sbuf[:, at] = (pert.astype(jnp.float32) * weight).astype(jnp.bfloat16)

    gram = lax.dot_general(
        ybuf[...], sbuf[...], (((1,), (1,)), ((), ())), preferred_element_type=jnp.float32
    )
    return gram[:members], jnp.sum(gram[members:], axis=0, keepdims=True)


def on_diagonal(size):
    return lax.broadcasted_iota(jnp.int32, (size, size), 0) == lax.broadcasted_iota(
        jnp.int32, (size, size), 1
    )


def sums_body(lists, meta, *refs, for_self, blocks_dev, width):
    tiles, (low, own, high) = refs[:6], refs[6:9]
    outs = refs[9:-4]
    raw, sems, ybuf, sbuf = refs[-4:]
    owner = meta[0] if for_self else 1 - meta[0]
    block = pl.program_id(0)
    blocks = raw.shape[0]

    @pl.when(block == 0)
    def _():
        for early in range(AHEAD):
            fetch(lists, meta, owner, early, tiles, raw, sems, blocks_dev, width)

    @pl.when(block + AHEAD < blocks)
    def _():
        fetch(lists, meta, owner, block + AHEAD, tiles, raw, sems, blocks_dev, width)

    matrix, rhs = local_gram(
        lists, meta, owner, block, raw, sems, low, own, high, ybuf, sbuf, blocks_dev, width
    )
    members = matrix.shape[0]
    if for_self:
        outs[0][0] = matrix
        outs[1][0] = jnp.broadcast_to(rhs, outs[1].shape[1:])
        return
    groups = members // ROWS
    diagonal = jnp.sum(jnp.where(on_diagonal(members), matrix, 0.0), axis=0, keepdims=True)
    matrix = 0.5 * (matrix + matrix.T)
    lane = lax.broadcasted_iota(jnp.int32, (ROWS, members), 1)
    packed = [matrix[:ROWS]]
    for group in range(1, groups // 2):
        filled = pltpu.roll(matrix[members - group * ROWS :][:ROWS], group * ROWS, 1)
        packed.append(
            jnp.where(lane < group * ROWS, filled, matrix[group * ROWS : (group + 1) * ROWS])
        )
    middle = matrix[members // 2 : members // 2 + ROWS, members // 2 :]
    last = [jnp.concatenate([middle[ROWS // 2 :], middle[: ROWS // 2]], axis=1)]
    last += [part.astype(jnp.float32) for part in parts3(rhs) + parts3(diagonal)]
    last.append(jnp.zeros((ROWS // 2 - 6, members), jnp.float32))
    packed.append(jnp.concatenate(last, axis=0))
    first = 0
    for out, size in zip(outs, SUMS):

        @pl.when((block >= first) & (block < first + size))
        def _(out=out):
            for group, rows in enumerate(packed):
                out[0, pl.ds(group * ROWS, ROWS), :] = rows.astype(jnp.bfloat16)

        first += size


def partial_sums(lists, meta, tiles, tables, for_self, blocks_dev, width):
    nloc, count = lists.shape
    half = count // 2
    members = 2 * tiles[0].shape[0]
    span = nloc * width
    table_spec = pl.BlockSpec(tables[0].shape, lambda i, *_: (0, 0))
    if for_self:
        shapes = [(half, members, members), (half, 8, members)]
        kind = jnp.float32
        out_specs = [pl.BlockSpec((1, *shape[1:]), lambda i, *_: (i, 0, 0)) for shape in shapes]
    else:
        shapes = [(size, members // 2 + ROWS, members) for size in SUMS]
        kind = jnp.bfloat16
        out_specs = [
            pl.BlockSpec(
                (1, *shape[1:]),
                lambda i, *_, first=sum(SUMS[:k]), size=SUMS[k]: (
                    jnp.clip(i - first, 0, size - 1), 0, 0,
                ),
            )
            for k, shape in enumerate(shapes)
        ]
    return pl.pallas_call(
        functools.partial(sums_body, for_self=for_self, blocks_dev=blocks_dev, width=width),
        grid_spec=pltpu.PrefetchScalarGridSpec(
            num_scalar_prefetch=2,
            grid=(half,),
            in_specs=[pl.BlockSpec(memory_space=pl.ANY)] * 6 + [table_spec] * 3,
            out_specs=out_specs,
            scratch_shapes=[
                pltpu.VMEM((half, members, span), jnp.bfloat16),
                pltpu.SemaphoreType.DMA((half,)),
                pltpu.VMEM((members + ROWS, span), jnp.bfloat16),
                pltpu.VMEM((members, span), jnp.bfloat16),
            ],
        ),
        out_shape=[jax.ShapeDtypeStruct(shape, kind) for shape in shapes],
        cost_estimate=pl.CostEstimate(
            flops=2 * half * members * members * span,
            bytes_accessed=2 * members * half * span,
            transcendentals=0,
        ),
        compiler_params=pltpu.CompilerParams(vmem_limit_bytes=20 << 20),
        name="sums_self" if for_self else "sums_send",
    )(lists, meta, *tiles, *tables)


def analysis_body(meta, mine, theirs, ours, our_rhs, received, *refs, width):
    kept, sent, ubuf, xbuf, mbuf = refs[-5:]
    rows = mine.shape[1]
    members = 2 * rows

    matrix = ours[0]
    rhs = our_rhs[0, pl.ds(0, 1), :]
    groups = members // ROWS
    ubuf[pl.ds(0, ROWS), :] = received[0, pl.ds(0, ROWS), :].astype(jnp.float32)
    for group in range(1, groups // 2):
        piece = received[0, pl.ds(group * ROWS, ROWS), :].astype(jnp.float32)
        ubuf[pl.ds(group * ROWS, ROWS), :] = piece
        ubuf[pl.ds(members - group * ROWS, ROWS), :] = pltpu.roll(
            piece, members - group * ROWS, 1
        )
    last = received[0, pl.ds(members // 2, ROWS), :].astype(jnp.float32)
    step = ROWS // 2
    ubuf[pl.ds(members // 2, step), pl.ds(rows, rows)] = last[:step, rows:]
    ubuf[pl.ds(members // 2 + step, step), pl.ds(rows, rows)] = last[:step, :rows]
    rhs = rhs + jnp.sum(last[step : step + 3], axis=0, keepdims=True)
    upper = ubuf[...]
    block_row = lax.div(lax.broadcasted_iota(jnp.int32, (members, members), 0), ROWS)
    block_col = lax.div(lax.broadcasted_iota(jnp.int32, (members, members), 1), ROWS)
    other = jnp.where(block_row <= block_col, upper, upper.T)
    diagonal = on_diagonal(members)
    other = jnp.where(diagonal, jnp.sum(last[step + 3 : step + 6], axis=0, keepdims=True), other)
    matrix = matrix + other
    matrix = matrix + jnp.where(diagonal, members - 1.0, 0.0)
    trace = jnp.sum(
        jnp.sum(jnp.where(diagonal, matrix, 0.0), axis=0, keepdims=True), axis=1, keepdims=True
    )
    scale = trace / members
    iterate = matrix / scale
    eye15 = jnp.where(diagonal, 1.5, 0.0)
    inverse_root = eye15 - 0.5 * iterate
    factor = split(inverse_root)
    iterate = dot3(factor, split(iterate))
    for step in range(1, NSTEPS):
        root_parts = split(inverse_root)
        iterate_parts = split(iterate)
        factor = split(eye15 - 0.5 * dot3(iterate_parts, root_parts))
        if step + 1 < NSTEPS:
            iterate = dot3(factor, iterate_parts)
        inverse_root = dot3(root_parts, factor)
    root_parts = split(inverse_root)
    shift = jnp.broadcast_to(rhs, (ROWS, members))
    shift = dot3(split(shift), root_parts)
    shift = dot3(split(shift), root_parts)[:1] / scale
    trans = (jnp.sqrt((members - 1.0) / scale) * inverse_root + shift).astype(jnp.bfloat16)

    layers = mine.shape[0]
    for layer in range(layers):
        at = pl.ds(layer * width, width)
        first = mine[layer].astype(jnp.float32)
        second = theirs[layer].astype(jnp.float32)
        mean = (
            jnp.sum(first, axis=0, keepdims=True) + jnp.sum(second, axis=0, keepdims=True)
        ) / members
        mbuf[:, at] = mean
        xbuf[pl.ds(0, rows), at] = (first - mean).astype(jnp.bfloat16)
        xbuf[pl.ds(rows, rows), at] = (second - mean).astype(jnp.bfloat16)
    result = (dot(trans, xbuf[...]) + mbuf[...]).astype(jnp.bfloat16)
    for layer in range(layers):
        at = slice(layer * width, (layer + 1) * width)
        kept[layer] = result[:rows, at]
        sent[layer] = result[rows:, at]


def analyse(meta, mine, theirs, ours, our_rhs, received, output, first, size, skipped, width):
    layers, rows, cols = mine.shape
    members = 2 * rows
    half = cols // 2 // width
    flops = 2 * size * members * members * (18 * members + layers * width)

    def mine_at(i, meta):
        return (0, 0, meta[0] * half + first + i)

    tile_block = (layers, rows, width)
    in_specs = [
        pl.BlockSpec(tile_block, mine_at),
        pl.BlockSpec(tile_block, lambda i, *_: (0, 0, first + i)),
        pl.BlockSpec((1, *ours.shape[1:]), lambda i, *_: (first + i, 0, 0)),
        pl.BlockSpec((1, *our_rhs.shape[1:]), lambda i, *_: (first + i, 0, 0)),
        pl.BlockSpec((1, *received.shape[1:]), lambda i, *_: (first - skipped + i, 0, 0)),
    ]
    operands = [mine, theirs, ours, our_rhs, received]
    aliases = {}
    if output is not None:
        in_specs.append(pl.BlockSpec(memory_space=pl.ANY))
        aliases = {1 + len(operands): 0}
        operands.append(output)
    return pl.pallas_call(
        functools.partial(analysis_body, width=width),
        grid_spec=pltpu.PrefetchScalarGridSpec(
            num_scalar_prefetch=1,
            grid=(size,),
            in_specs=in_specs,
            out_specs=[
                pl.BlockSpec(tile_block, mine_at),
                pl.BlockSpec(tile_block, lambda i, *_: (0, 0, i)),
            ],
            scratch_shapes=[
                pltpu.VMEM((members, members), jnp.float32),
                pltpu.VMEM((members, layers * width), jnp.bfloat16),
                pltpu.VMEM((1, layers * width), jnp.float32),
            ],
        ),
        out_shape=[
            jax.ShapeDtypeStruct(mine.shape, jnp.bfloat16),
            jax.ShapeDtypeStruct((layers, rows, size * width), jnp.bfloat16),
        ],
        input_output_aliases=aliases,
        cost_estimate=pl.CostEstimate(
            flops=flops, bytes_accessed=size * 8 * rows * layers * width, transcendentals=0
        ),
        compiler_params=pltpu.CompilerParams(vmem_limit_bytes=20 << 20),
        name="analyse",
    )(meta, *operands)


def place_body(piece, output, placed, sem, *, first, width):
    mem = lax.axis_index("mem")
    start = pl.multiple_of((1 - mem) * (placed.shape[2] // 2) + first * width, width)
    copy = pltpu.make_async_copy(piece, placed.at[:, :, pl.ds(start, piece.shape[2])], sem)
    copy.start()
    copy.wait()


def place(piece, output, first, width):
    return pl.pallas_call(
        functools.partial(place_body, first=first, width=width),
        in_specs=[pl.BlockSpec(memory_space=pl.ANY)] * 2,
        out_specs=pl.BlockSpec(memory_space=pl.ANY),
        scratch_shapes=[pltpu.SemaphoreType.DMA],
        out_shape=jax.ShapeDtypeStruct(output.shape, output.dtype),
        input_output_aliases={1: 0},
        cost_estimate=pl.CostEstimate(
            flops=0, bytes_accessed=4 * piece.size, transcendentals=0
        ),
        compiler_params=pltpu.CompilerParams(vmem_limit_bytes=2 << 20),
        name="place",
    )(piece, output)


def per_device(
    prior_members,
    members_in_reading_space,
    measured_values,
    obs_precision_weights,
    valid_reading_numbers,
    neighbour_lists,
):
    tile_no = lax.axis_index("tile")
    member_no = lax.axis_index("mem")
    tiles = lax.axis_size("tile")
    mems = lax.axis_size("mem")
    both = ("mem", "tile")
    swap = [(0, 1), (1, 0)]
    from_low = side_pairs(tiles, mems, -1)
    from_high = side_pairs(tiles, mems, 1)
    blocks_dev = valid_reading_numbers.shape[0]
    width = members_in_reading_space.shape[1] // blocks_dev
    cols = prior_members.shape[2]

    mine = jnp.transpose(prior_members, (1, 0, 2))
    lists = neighbour_lists.T
    meta = jnp.stack([member_no, tile_no]).astype(jnp.int32)

    obs = members_in_reading_space
    other_set = pick_half(obs, True)
    swapped = lax.ppermute(other_set, "mem", swap)
    own_set = pick_half(obs, False, other_set)
    low_own = lax.ppermute(own_set, both, from_low)
    high_own = lax.ppermute(own_set, both, from_high)
    half = cols // 2
    outgoing = lax.dynamic_slice_in_dim(mine, (1 - member_no) * half, half, 2)
    theirs = lax.ppermute(outgoing, "mem", swap)
    low_other = lax.ppermute(swapped, both, from_low)
    high_other = lax.ppermute(swapped, both, from_high)
    tiles_held = (low_own, low_other, own_set, swapped, high_own, high_other)
    slots = jnp.arange(width, dtype=jnp.int32)
    valid = slots[None, :] < valid_reading_numbers[:, None]
    weight = jnp.where(valid, obs_precision_weights.reshape(blocks_dev, width), 0.0)
    table = jnp.concatenate([measured_values.reshape(blocks_dev, width), weight], axis=0)
    table_low = lax.ppermute(table, both, from_low)
    table_high = lax.ppermute(table, both, from_high)
    tables = (table_low, table, table_high)

    sums = partial_sums(lists, meta, tiles_held, tables, False, blocks_dev, width)
    received = []
    for piece in sums:
        received.append(lax.ppermute(piece, "mem", swap))
    ours, our_rhs = partial_sums(lists, meta, tiles_held, tables, True, blocks_dev, width)
    output = None
    arrived = []
    for k, size in enumerate(PIECES):
        first = sum(PIECES[:k])
        late = first >= SUMS[0]
        output, sent = analyse(
            meta, mine, theirs, ours, our_rhs, received[late], output, first, size,
            SUMS[0] if late else 0, width,
        )
        arrived.append(lax.ppermute(sent, "mem", swap))
    for k, piece in enumerate(arrived):
        output = place(piece, output, sum(PIECES[:k]), width)
    return jnp.transpose(output, (1, 0, 2))


def solution(mesh):
    in_specs = (
        P("mem", None, "tile"),
        P("mem", "tile"),
        P("tile"),
        P("tile"),
        P("tile"),
        P("tile", None),
    )
    out_specs = P("mem", None, "tile")

    return jax.shard_map(
        per_device, mesh=mesh, in_specs=in_specs, out_specs=out_specs, check_vma=False
    )
```
